512 devices in a mesh: tile: 64 (over y, z_lo, x), fsdp: 8 (over z_hi, core).
Axes of the slice: x: 4, y: 8, z: 8 (z_hi: 4, z_lo: 2; z = z_hi * 2 + z_lo), core: 2. Of those that a mesh axis runs over, the one named last changes fastest.
Arguments:
- cap_in: bfloat16 [8, 64, 256, 128], P('fsdp', 'tile'), may hold values from -16 to 16
- conv1_weight: bfloat16 [3, 3, 128, 256], P(None, None, None, 'fsdp'), may hold values from -0.1875 to 0.1875
- conv2_weight: bfloat16 [3, 3, 256, 256], P(None, None, None, 'fsdp'), may hold values from -0.125 to 0.125
- out_grad: bfloat16 [8, 64, 256, 256], P('fsdp', 'tile'), may hold values from -6 to 6
Outputs:
- cap_out: bfloat16 [8, 64, 256, 256], P('fsdp', 'tile')
- in_grad: bfloat16 [8, 64, 256, 128], P('fsdp', 'tile')
- conv1_grad: float32 [256, 3, 3, 128], P('fsdp', None, None, 'tile')
- conv2_grad: float32 [256, 3, 3, 256], P('fsdp', None, None, 'tile')
The draws below stay inside these ranges and needn't reach their ends.
All inputs are finite; a program needn't handle non-finite values.
Results may differ from the reference program's by a relative error of at most 0.0049.
Values may be sent and summed in bfloat16 or wider, within the bound.
A program may use at most 64 MiB of HBM per device.

```python
import jax
import jax.numpy as jnp
from jax import lax

CIN = 128
CH = 256
COLS = 256
SIDE = 64
SAMPLES = 8


def raised(result, own_key, source, target, shards_of, factor):
    def block_of(position):
        return (jnp.arange(result.shape[position]) // (result.shape[position] // shards_of)).reshape((-1,) + (1,) * (result.ndim - 1 - position))

    first = jax.random.permutation(own_key, shards_of)[block_of(target)]
    other_side = (block_of(target) + shards_of // 2) % shards_of
    return jnp.where((block_of(source) == first) | (block_of(source) == other_side), factor * result, result)


def steps_of(rng, extent, shards, smallest, high):
    def one(dim, blocks):
        steps = jax.random.uniform(jax.random.fold_in(jax.random.fold_in(rng, 6), dim), (blocks,), jnp.float32, smallest / len(shards), high / len(shards))
        return jnp.repeat(jnp.exp(steps), extent[dim] // blocks).reshape((-1,) + (1,) * (len(extent) - dim - 1))

    factor_of = one(*shards[0])
    for cut in shards[1:]:
        factor_of = factor_of * one(*cut)
    return factor_of


def bell_draw(stream_key, shape, spread, limit, pieces=(), kind=jnp.bfloat16):
    result = jax.random.normal(stream_key, shape, jnp.float32) * spread
    if len(pieces) > 0:
        result = steps_of(stream_key, shape, pieces, -0.22, 0.18) * result
    return jnp.clip(result, min=-limit, max=limit).astype(kind)


def noise_with(key, dims, width, bound, cuts, heavy, kind=jnp.bfloat16):
    values = width * jax.random.normal(key, dims, jnp.float32)
    if cuts:
        values = values * steps_of(key, dims, cuts, -0.22, 0.18)
    return jnp.clip(raised(values, jax.random.fold_in(key, 3), *heavy), -bound, bound).astype(kind)


def setup_inputs(seed: int = 0) -> dict:
    streams_of = jax.random.split(jax.random.key(seed), 5)
    return {
        "cap_in": noise_with(streams_of[0], (SAMPLES, SIDE, COLS, CIN), 1.0, 16.0, ((0, 8), (1, 64)), (1, 3, 64, 4.0)),
        "conv1_weight": bell_draw(streams_of[1], (3, 3, CIN, CH), (9 * CIN) ** -0.5, 0.1875, ((3, 8),)),
        "conv2_weight": bell_draw(streams_of[2], (3, 3, CH, CH), (9 * CH) ** -0.5, 0.125, ((3, 8),)),
        "out_grad": bell_draw(streams_of[3], (SAMPLES, SIDE, COLS, CH), 1.0, 6.0, ((0, 8), (1, 64))),
    }


def padded_grid(values):
    return jnp.pad(values.astype(jnp.float32), ((1, 1), (1, 1), (0, 0)))

def conv_grid(padded, weight):
    height = padded.shape[0] - 2
    breadth = padded.shape[1] - 2
    summed = jnp.zeros((height * breadth, weight.shape[3]), jnp.float32)
    for vertical in range(3):
        for lateral in range(3):
            window = padded[vertical:vertical + height, lateral:lateral + breadth].reshape(height * breadth, weight.shape[2])
            summed = summed + jnp.dot(window, weight[vertical, lateral], preferred_element_type=jnp.float32, precision=lax.Precision.HIGHEST)
    return summed.reshape(height, breadth, weight.shape[3])

def flipped_weight(weight):
    return jnp.transpose(weight[::-1, ::-1], (0, 1, 3, 2))

def weight_terms(padded, cotangent):
    height = cotangent.shape[0]
    breadth = cotangent.shape[1]
    flat_grad = cotangent.reshape(height * breadth, cotangent.shape[2]).T
    stacked = []
    for vertical in range(3):
        rowwise = []
        for lateral in range(3):
            window = padded[vertical:vertical + height, lateral:lateral + breadth].reshape(height * breadth, padded.shape[2])
            rowwise.append(jnp.dot(flat_grad, window, preferred_element_type=jnp.float32, precision=lax.Precision.HIGHEST))
        stacked.append(jnp.stack(rowwise, axis=1))
    return jnp.stack(stacked, axis=1)

def reference(cap_in, conv1_weight, conv2_weight, out_grad):
    weight_first = conv1_weight.astype(jnp.float32)
    weight_second = conv2_weight.astype(jnp.float32)

    def one_sample(sample_pair):
        sample_in, sample_grad = sample_pair
        input_pad = padded_grid(sample_in)
        pre_first = conv_grid(input_pad, weight_first)
        hidden = lax.optimization_barrier(jax.nn.silu(pre_first).astype(jnp.bfloat16))
        hidden_pad = padded_grid(hidden)
        block_out = conv_grid(hidden_pad, weight_second).astype(jnp.bfloat16)
        hidden_grad = conv_grid(padded_grid(sample_grad), flipped_weight(weight_second))
        sigmoid = jax.nn.sigmoid(pre_first)
        pre_grad = lax.optimization_barrier((hidden_grad * sigmoid * (1.0 + pre_first * (1.0 - sigmoid))).astype(jnp.bfloat16))
        input_grad = conv_grid(padded_grid(pre_grad), flipped_weight(weight_first)).astype(jnp.bfloat16)
        second_terms = weight_terms(hidden_pad, sample_grad.astype(jnp.float32))
        first_terms = weight_terms(input_pad, pre_grad.astype(jnp.float32))
        return (block_out, input_grad, first_terms, second_terms)
    block_out, input_grad, first_terms, second_terms = lax.map(one_sample, (cap_in, out_grad))
    grad_scale = jnp.float32(1.0) / jnp.sqrt(jnp.float32(SAMPLES * SIDE * COLS))
    return (block_out, input_grad, lax.optimization_barrier(jnp.sum(first_terms, axis=0)) * grad_scale, lax.optimization_barrier(jnp.sum(second_terms, axis=0)) * grad_scale)
```

```python
import math

import jax
import jax.numpy as jnp
from jax import lax
from jax.experimental import pallas as pl
from jax.experimental.pallas import tpu as pltpu
from jax.sharding import PartitionSpec as P

MESH = pl.DeviceIdType.MESH
F32 = jnp.float32
BF16 = jnp.bfloat16
NX, NY, NZ = 4, 8, 8
TILES, SHARDS = 64, 8
VMEM_BYTES = 60 * 1024 * 1024


def position():
    tile = lax.axis_index("tile")
    fsdp = lax.axis_index("fsdp")
    return dict(x=tile % 4, zl=(tile // 4) % 2, y=tile // 8, zh=fsdp // 2, core=fsdp % 2, tile=tile, fsdp=fsdp)


def device(p, **moved):
    q = {**p, **moved}
    return ((q["y"] * 2 + q["zl"]) * 4 + q["x"], q["zh"] * 2 + q["core"])


def remote(src, dst, sems, index, target):
    send, recv = sems
    return pltpu.make_async_remote_copy(
        src_ref=src, dst_ref=dst, send_sem=send.at[index], recv_sem=recv.at[index],
        device_id=target, device_id_type=MESH,
    )


def meet(targets):
    barrier = pltpu.get_barrier_semaphore()
    for target in targets:
        pl.semaphore_signal(barrier, inc=1, device_id=target, device_id_type=MESH)
    pl.semaphore_wait(barrier, len(targets))


def gather_kernel(cap, grad, shard, hcap, hgrad, whole, hs, hr, zs, zr, ps, pr, cs, cr, own):
    p = position()
    tile, fsdp = p["tile"], p["fsdp"]
    role = (p["x"] + 2 * p["y"]) % 4
    sibling = device(p, core=1 - p["core"])
    xup, xdown = device(p, x=(p["x"] + 1) % 4), device(p, x=(p["x"] + 3) % 4)
    yup, ydown = device(p, y=(p["y"] + 1) % 8), device(p, y=(p["y"] + 7) % 8)
    zpeers = [device(p, zh=(p["zh"] + d) % 4) for d in (1, 2, 3)]
    rows = [((tile + d) % TILES, fsdp) for d in (2, 1, TILES - 1, TILES - 2)]
    meet([sibling, xup, xdown, yup, ydown] + zpeers + rows)

    first = []
    for d, target in enumerate(zpeers):
        first.append(remote(shard.at[role], whole.at[fsdp * 4 + role], (zs, zr), d, target))
    for copy in first:
        copy.start()
    halos = [
        remote(grad, hgrad.at[0], (hs, hr), 4, rows[1]),
        remote(grad, hgrad.at[1], (hs, hr), 5, rows[2]),
        remote(cap, hcap.at[1], (hs, hr), 1, rows[1]),
        remote(cap, hcap.at[2], (hs, hr), 2, rows[2]),
        remote(cap, hcap.at[0], (hs, hr), 0, rows[0]),
        remote(cap, hcap.at[3], (hs, hr), 3, rows[3]),
    ]
    for copy in halos:
        copy.start()
    mine = pltpu.make_async_copy(shard, whole.at[pl.ds(fsdp * 4, 4)], own)
    mine.start()
    pair = [remote(shard, whole.at[pl.ds(fsdp * 4, 4)], (cs, cr), 12, sibling)]
    pair[0].start()

    second = []
    for d in range(3):
        first[d].wait_recv()
        source = ((p["zh"] + 3 - d) % 4) * 2 + p["core"]
        slot = whole.at[source * 4 + role]
        sends = [(xup, 0), (xdown, 1), (yup if d < 2 else ydown, 2)]
        for target, k in sends:
            copy = remote(slot, slot, (ps, pr), d * 3 + k, target)
            copy.start()
            second.append(copy)
        copy = remote(slot, slot, (cs, cr), d * 4 + 3, sibling)
        copy.start()
        pair.append(copy)
    for d in range(3):
        source = ((p["zh"] + 3 - d) % 4) * 2 + p["core"]
        for k, step in ((0, 3), (1, 1), (2, 2)):
            second[d * 3 + k].wait_recv()
            slot = whole.at[source * 4 + (role + step) % 4]
            copy = remote(slot, slot, (cs, cr), d * 4 + k, sibling)
            copy.start()
            pair.append(copy)
    mine.wait()
    for copy in pair + halos:
        copy.wait()
    for copy in first + second:
        copy.wait_send()


def gather(cap, grad, shard):
    anywhere = pl.BlockSpec(memory_space=pl.ANY)
    dma = pltpu.SemaphoreType.DMA
    return pl.pallas_call(
        gather_kernel,
        out_shape=(
            jax.ShapeDtypeStruct((4,) + cap.shape, BF16),
            jax.ShapeDtypeStruct((2,) + grad.shape, BF16),
            jax.ShapeDtypeStruct((SHARDS * 4,) + shard.shape[1:], BF16),
        ),
        in_specs=[anywhere, anywhere, pl.BlockSpec(memory_space=pltpu.VMEM)],
        out_specs=(anywhere, anywhere, anywhere),
        scratch_shapes=[
            dma((6,)), dma((6,)), dma((3,)), dma((3,)), dma((9,)), dma((9,)), dma((13,)), dma((13,)), dma(()),
        ],
        compiler_params=pltpu.CompilerParams(collective_id=0, has_side_effects=True),
        name="gather",
    )(cap, grad, shard)


def dot(a, b):
    return jnp.dot(a, b, preferred_element_type=F32)


def dot_nt(a, b):
    return lax.dot_general(a, b, (((1,), (1,)), ((), ())), preferred_element_type=F32)


def moved(v, step):
    n = v.shape[0]
    pixel = lax.broadcasted_iota(jnp.int32, v.shape, 0)
    if step == 1:
        return jnp.where(pixel == 0, 0.0, pltpu.roll(v, 1, 0))
    return jnp.where(pixel == n - 1, 0.0, pltpu.roll(v, n - 1, 0))


def joined(first, middle, last):
    return middle + moved(first, 1) + moved(last, -1)


def compute_kernel(flags, cap, hcap, grad, hgrad, w1, w2, order_o, order_c1, order_c2,
                   cap_out, pre_grad, keep1, give1, keep2, give2,
                   x5, xcat, hcat, gcat, pre):
    def live(v, r):
        return jnp.where(flags[r + 2] > 0, v, jnp.zeros_like(v))

    x5[0] = live(hcap[0], -2)
    x5[1] = live(hcap[1], -1)
    x5[2] = cap[...]
    x5[3] = live(hcap[2], 1)
    x5[4] = live(hcap[3], 2)
    gcat[0] = live(hgrad[0], -1)
    gcat[1] = grad[...]
    gcat[2] = live(hgrad[1], 1)
    for r in range(3):
        for a in range(3):
            xcat[:, a * 128 : (a + 1) * 128] = x5[r + a]
        y = [dot_nt(xcat[...], w1[:, b * 384 : (b + 1) * 384]) for b in range(3)]
        v = joined(*y)
        if r == 1:
            pre[...] = v
        h = (v * jax.nn.sigmoid(v)).astype(BF16)
        hcat[:, r * 256 : (r + 1) * 256] = h if r == 1 else live(h, r - 1)

    y = []
    for b in range(3):
        total = None
        for a in range(3):
            at = ((2 - b) * 3 + (2 - a)) * 256
            part = dot(gcat[a], w2[:, at : at + 256])
            total = part if total is None else total + part
        y.append(total)
    hidden_grad = joined(*y)
    v = pre[...]
    sig = jax.nn.sigmoid(v)
    pg = (hidden_grad * sig * (1.0 + v * (1.0 - sig))).astype(BF16)
    pre_grad[...] = pg

    def terms(cot, rows, order_c, keep, give, block):
        g = dot(cot, order_o[...])
        shifted = jnp.concatenate([moved(g, -1), g, moved(g, 1)], axis=1).astype(BF16)
        for a in range(3):
            left = dot_nt(order_c[...], rows(a)).astype(BF16)
            t = dot(left, shifted)
            for b in range(3):
                for n in range(t.shape[0] // block):
                    part = t[n * block : (n + 1) * block, b * 256 : (b + 1) * 256]
                    keep[n, a * 3 + b] = part[:, :128]
                    give[n, a * 3 + b] = part[:, 128:].astype(BF16)

    terms(pg, lambda a: x5[a + 1], order_c1, keep1, give1, 16)
    terms(grad[...], lambda a: hcat[:, a * 256 : (a + 1) * 256], order_c2, keep2, give2, 64)

    y = [dot_nt(hcat[...], w2[:, b * 768 : (b + 1) * 768]) for b in range(3)]
    cap_out[...] = joined(*y).astype(BF16)


def compute(flags, cap, hcap, grad, hgrad, w1, w2, order_o, order_c1, order_c2):
    vmem = pl.BlockSpec(memory_space=pltpu.VMEM)
    return pl.pallas_call(
        compute_kernel,
        out_shape=(
            jax.ShapeDtypeStruct((256, 256), BF16),
            jax.ShapeDtypeStruct((256, 256), BF16),
            jax.ShapeDtypeStruct((8, 9, 16, 128), F32),
            jax.ShapeDtypeStruct((8, 9, 16, 128), BF16),
            jax.ShapeDtypeStruct((4, 9, 64, 128), F32),
            jax.ShapeDtypeStruct((4, 9, 64, 128), BF16),
        ),
        in_specs=[pl.BlockSpec(memory_space=pltpu.SMEM)] + [vmem] * 9,
        out_specs=(vmem,) * 6,
        scratch_shapes=[
            pltpu.VMEM((5, 256, 128), BF16),
            pltpu.VMEM((256, 384), BF16),
            pltpu.VMEM((256, 768), BF16),
            pltpu.VMEM((3, 256, 256), BF16),
            pltpu.VMEM((256, 256), F32),
        ],
        compiler_params=pltpu.CompilerParams(vmem_limit_bytes=VMEM_BYTES),
        name="compute",
    )(flags, cap, hcap, grad, hgrad, w1, w2, order_o, order_c1, order_c2)


def reduce_kernel(scale, keep1, give1, keep2, give2, pre_grad, result, hpre,
                  rc1, rc2, s1, s2, r1a, r2a, k1, k2, s1b, s2b, r1b, r2b, kc, sc, rcz,
                  hs, hr, cs, cr, as_, ar, bs, br, zs, zr):
    p = position()
    tile, fsdp, x, y = p["tile"], p["fsdp"], p["x"], p["y"]
    sibling = device(p, core=1 - p["core"])
    xpeers = [device(p, x=(x + d) % 4) for d in range(1, 4)]
    ypeers = [device(p, y=(y + d) % 8) for d in range(1, 8)]
    z = p["zh"] * 2 + p["zl"]
    zto = [(z + d) % 8 for d in range(1, 8)]
    zpeers = [device(p, zh=t // 2, zl=t % 2) for t in zto]
    rows = [((tile + 1) % TILES, fsdp), ((tile + TILES - 1) % TILES, fsdp)]
    meet([sibling] + xpeers + ypeers + zpeers + rows)

    pair = [remote(give2, rc2, (cs, cr), 0, sibling), remote(give1, rc1, (cs, cr), 1, sibling)]
    halos = [remote(pre_grad, hpre.at[0], (hs, hr), 0, rows[0]), remote(pre_grad, hpre.at[1], (hs, hr), 1, rows[1])]
    for copy in pair:
        copy.start()

    pair[0].wait_recv()
    sent = []
    for d in range(3):
        to = (x + d + 1) % 4
        s2[to] = (keep2[to] + rc2[to].astype(F32)).astype(BF16)
        copy = remote(s2.at[to], r2a.at[d], (as_, ar), d, xpeers[d])
        copy.start()
        sent.append(copy)
    pair[1].wait_recv()
    for d in range(7):
        to = (y + d + 1) % 8
        s1[to] = (keep1[to] + rc1[to].astype(F32)).astype(BF16)
        copy = remote(s1.at[to], r1a.at[d], (as_, ar), 3 + d, ypeers[d])
        copy.start()
        sent.append(copy)
    for copy in halos:
        copy.start()

    total = keep2[x] + rc2[x].astype(F32)
    for d in range(3):
        sent[d].wait_recv()
        total = total + r2a[d].astype(F32)
    for n in range(8):
        k2[n] = total[:, n * 8 : (n + 1) * 8]
        s2b[n] = k2[n].astype(BF16)
    second = []
    for d in range(7):
        copy = remote(s2b.at[(y + d + 1) % 8], r2b.at[d], (bs, br), d, ypeers[d])
        copy.start()
        second.append(copy)
    total = keep1[y] + rc1[y].astype(F32)
    for d in range(7):
        sent[3 + d].wait_recv()
        total = total + r1a[d].astype(F32)
    for n in range(4):
        k1[n] = total[:, n * 4 : (n + 1) * 4]
        s1b[n] = k1[n].astype(BF16)
    for d in range(3):
        copy = remote(s1b.at[(x + d + 1) % 4], r1b.at[d], (bs, br), 7 + d, xpeers[d])
        copy.start()
        second.append(copy)

    t2 = k2[y]
    for d in range(7):
        second[d].wait_recv()
        t2 = t2 + r2b[d].astype(F32)
    t1 = k1[x]
    for d in range(3):
        second[7 + d].wait_recv()
        t1 = t1 + r1b[d].astype(F32)
    for n in range(2):
        kc[n, :, 0:4] = t2[:, n * 4 : (n + 1) * 4]
        kc[n, :, 4:6] = t1[:, n * 2 : (n + 1) * 2]
        kc[n, :, 6:8] = jnp.zeros((9, 2, 128), F32)
        sc[n] = kc[n].astype(BF16)
    third = []
    for d in range(7):
        copy = remote(sc.at[zto[d] % 2], rcz.at[d], (zs, zr), d, zpeers[d])
        copy.start()
        third.append(copy)
    total = kc[p["zl"]]
    for d in range(7):
        third[d].wait_recv()
        total = total + rcz[d].astype(F32)
    result[...] = total * scale
    for copy in pair + sent + second + third:
        copy.wait_send()
    for copy in halos:
        copy.wait()


def reduce(scale, keep1, give1, keep2, give2, pre_grad):
    vmem = pl.BlockSpec(memory_space=pltpu.VMEM)
    anywhere = pl.BlockSpec(memory_space=pl.ANY)
    dma = pltpu.SemaphoreType.DMA

    def kernel(*refs):
        return reduce_kernel(scale, *refs)

    return pl.pallas_call(
        kernel,
        out_shape=(
            jax.ShapeDtypeStruct((9, 8, 128), F32),
            jax.ShapeDtypeStruct((2, 256, 256), BF16),
        ),
        in_specs=[vmem] * 4 + [anywhere],
        out_specs=(vmem, anywhere),
        scratch_shapes=[
            pltpu.VMEM((8, 9, 16, 128), BF16),
            pltpu.VMEM((4, 9, 64, 128), BF16),
            pltpu.VMEM((8, 9, 16, 128), BF16),
            pltpu.VMEM((4, 9, 64, 128), BF16),
            pltpu.VMEM((7, 9, 16, 128), BF16),
            pltpu.VMEM((3, 9, 64, 128), BF16),
            pltpu.VMEM((4, 9, 4, 128), F32),
            pltpu.VMEM((8, 9, 8, 128), F32),
            pltpu.VMEM((4, 9, 4, 128), BF16),
            pltpu.VMEM((8, 9, 8, 128), BF16),
            pltpu.VMEM((3, 9, 4, 128), BF16),
            pltpu.VMEM((7, 9, 8, 128), BF16),
            pltpu.VMEM((2, 9, 8, 128), F32),
            pltpu.VMEM((2, 9, 8, 128), BF16),
            pltpu.VMEM((7, 9, 8, 128), BF16),
            dma((2,)), dma((2,)), dma((2,)), dma((2,)), dma((10,)), dma((10,)),
            dma((10,)), dma((10,)), dma((7,)), dma((7,)),
        ],
        compiler_params=pltpu.CompilerParams(
            collective_id=1, has_side_effects=True, vmem_limit_bytes=VMEM_BYTES
        ),
        name="reduce",
    )(keep1, give1, keep2, give2, pre_grad)


def input_kernel(flags, pre_grad, hpre, w1, in_grad):
    rows = [
        jnp.where(flags[1] > 0, hpre[0], jnp.zeros_like(hpre[0])),
        pre_grad[...],
        jnp.where(flags[3] > 0, hpre[1], jnp.zeros_like(hpre[1])),
    ]
    y = []
    for b in range(3):
        total = None
        for a in range(3):
            at = ((2 - b) * 3 + (2 - a)) * 128
            part = dot(rows[a], w1[:, at : at + 128])
            total = part if total is None else total + part
        y.append(total)
    in_grad[...] = joined(*y).astype(BF16)


def input_grad(flags, pre_grad, hpre, w1):
    vmem = pl.BlockSpec(memory_space=pltpu.VMEM)
    return pl.pallas_call(
        input_kernel,
        out_shape=jax.ShapeDtypeStruct((256, 128), BF16),
        in_specs=[pl.BlockSpec(memory_space=pltpu.SMEM)] + [vmem] * 3,
        out_specs=vmem,
        compiler_params=pltpu.CompilerParams(vmem_limit_bytes=VMEM_BYTES),
        name="input_grad",
    )(flags, pre_grad, hpre, w1)


def flat_shard(weight):
    return jnp.transpose(weight, (3, 1, 0, 2)).reshape(weight.shape[3], -1)


def body(cap_in, conv1_weight, conv2_weight, out_grad):
    tile = lax.axis_index("tile")
    fsdp = lax.axis_index("fsdp")
    core, zh = fsdp % 2, fsdp // 2
    scale = 1.0 / math.sqrt(SHARDS * TILES * 256)
    cap = cap_in.reshape(256, 128)
    grad = out_grad.reshape(256, 256)
    row = tile + jnp.arange(-2, 3, dtype=jnp.int32)
    flags = ((row >= 0) & (row < TILES)).astype(jnp.int32)

    n = jnp.arange(256, dtype=jnp.int32)
    where = (n // 128 + core) % 2
    source_o = ((n % 128) // 32) * 64 + where * 32 + n % 32
    order_o = (n[:, None] == source_o[None, :]).astype(BF16)
    source_c2 = ((n // 8) % 8) * 32 + ((n // 4) % 2) * 16 + (n // 64) * 4 + n % 4
    order_c2 = (source_c2[:, None] == n[None, :]).astype(BF16)
    m = n[:128]
    source_c1 = (m // 16) * 16 + ((m // 2) % 2) * 8 + ((m // 4) % 4) * 2 + m % 2
    order_c1 = (source_c1[:, None] == m[None, :]).astype(BF16)

    shard = jnp.concatenate([flat_shard(conv1_weight), flat_shard(conv2_weight)], axis=1)
    hcap, hgrad, whole = gather(cap, grad, shard.reshape(4, 8, -1))
    whole = whole.reshape(256, -1)
    w1, w2 = whole[:, :1152], whole[:, 1152:]
    cap_out, pre_grad, keep1, give1, keep2, give2 = compute(
        flags, cap, hcap, grad, hgrad, w1, w2, order_o, order_c1, order_c2
    )
    result, hpre = reduce(scale, keep1, give1, keep2, give2, pre_grad)
    in_grad = input_grad(flags, pre_grad, hpre, w1)
    part = lax.dynamic_slice_in_dim(result, zh * 32, 32, axis=2)
    part = jnp.transpose(part, (2, 0, 1)).reshape(32, 3, 3, 8)
    return (
        cap_out.reshape(1, 1, 256, 256),
        in_grad.reshape(1, 1, 256, 128),
        part[..., 4:6],
        part[..., 0:4],
    )


def solution(mesh):
    placed = (
        P("fsdp", "tile", None, None),
        P(None, None, None, "fsdp"),
        P(None, None, None, "fsdp"),
        P("fsdp", "tile", None, None),
    )
    return jax.shard_map(
        body,
        mesh=mesh,
        in_specs=placed,
        out_specs=(
            P("fsdp", "tile", None, None),
            P("fsdp", "tile", None, None),
            P("fsdp", None, None, "tile"),
            P("fsdp", None, None, "tile"),
        ),
        check_vma=False,
    )
```

```python
import math

import jax
import jax.numpy as jnp
from jax import lax
from jax.experimental import pallas as pl
from jax.experimental.pallas import tpu as pltpu
from jax.sharding import PartitionSpec as P

MESH = pl.DeviceIdType.MESH
F32 = jnp.float32
BF16 = jnp.bfloat16
TILES = 64
VMEM_BYTES = 60 * 1024 * 1024
SCALE = 1.0 / math.sqrt(8 * 64 * 256)


def position():
    tile = lax.axis_index("tile")
    fsdp = lax.axis_index("fsdp")
    return dict(x=tile % 4, zl=(tile // 4) % 2, y=tile // 8, zh=fsdp // 2, core=fsdp % 2, tile=tile, fsdp=fsdp)


def device(p, **moved):
    q = {**p, **moved}
    return ((q["y"] * 2 + q["zl"]) * 4 + q["x"], q["zh"] * 2 + q["core"])


def remote(src, dst, sems, index, target):
    send, recv = sems
    return pltpu.make_async_remote_copy(
        src_ref=src, dst_ref=dst, send_sem=send.at[index], recv_sem=recv.at[index],
        device_id=target, device_id_type=MESH,
    )


def dot(a, b):
    return jnp.dot(a, b, preferred_element_type=F32)


def dot_nt(a, b):
    return lax.dot_general(a, b, (((1,), (1,)), ((), ())), preferred_element_type=F32)


def moved(v, step):
    n = v.shape[0]
    pixel = lax.broadcasted_iota(jnp.int32, v.shape, 0)
    if step == 1:
        return jnp.where(pixel == 0, 0.0, pltpu.roll(v, 1, 0))
    return jnp.where(pixel == n - 1, 0.0, pltpu.roll(v, n - 1, 0))


def joined(first, middle, last):
    return middle + moved(first, 1) + moved(last, -1)


def fused_kernel(cap, grad, w1, w2, cap_out, in_grad, result,
                 shard1, shard2, all1, all2, hcap, hgrad, hpre, x5, xcat, hcat, gcat, pre, pg,
                 keep1, keep2, give1, give2, rc1, rc2, s1, s2, r1a, r2a,
                 k1, k2, s1b, s2b, r1b, r2b, kc, sc, rcz,
                 own, hs, hr, zs, zr, ps, pr, cs, cr, es, er, as_, ar, bs, br, fs, fr):
    p = position()
    tile, fsdp, x, y, core = p["tile"], p["fsdp"], p["x"], p["y"], p["core"]
    role = (x + 2 * y) % 4
    sibling = device(p, core=1 - core)
    xpeers = [device(p, x=(x + d) % 4) for d in range(1, 4)]
    ypeers = [device(p, y=(y + d) % 8) for d in range(1, 8)]
    z = p["zh"] * 2 + p["zl"]
    zto = [(z + d) % 8 for d in range(1, 8)]
    zpeers = [device(p, zh=t // 2, zl=t % 2) for t in zto]
    zsame = [device(p, zh=(p["zh"] + d) % 4) for d in (1, 2, 3)]
    rows = [((tile + d) % TILES, fsdp) for d in (2, 1, TILES - 1, TILES - 2)]
    xup, xdown, yup, ydown = xpeers[0], xpeers[2], ypeers[0], ypeers[6]

    barrier = pltpu.get_barrier_semaphore()
    greeted = [sibling] + xpeers + ypeers + zpeers + rows
    for target in greeted:
        pl.semaphore_signal(barrier, inc=1, device_id=target, device_id_type=MESH)

    unit = (lax.broadcasted_iota(jnp.int32, (32, 32), 0) == lax.broadcasted_iota(jnp.int32, (32, 32), 1))
    unit = unit.astype(F32).astype(BF16)
    for weight, shard, c in ((w1, shard1, 128), (w2, shard2, 256)):
        for a in range(3):
            for b in range(3):
                at = (a * 3 + b) * c
                to = (b * 3 + a) * c
                flat = dot_nt(unit, weight[at : at + c, :])
                for q in range(4):
                    shard[q, :, to : to + c] = flat[q * 8 : (q + 1) * 8].astype(BF16)

    pl.semaphore_wait(barrier, len(greeted))

    sets = ((shard1, all1), (shard2, all2))
    first, second, pair, mine = [[], []], [[], []], [[], []], []

    def start(copy, group):
        copy.start()
        group.append(copy)

    def launch_weight(w):
        shard, whole = sets[w]
        for d in range(3):
            start(remote(shard.at[role], whole.at[fsdp * 4 + role], (zs, zr), (w, d), zsame[d]), first[w])
        start(remote(shard, whole.at[pl.ds(fsdp * 4, 4)], (cs, cr), (w, 12), sibling), pair[w])
        copy = pltpu.make_async_copy(shard, whole.at[pl.ds(fsdp * 4, 4)], own.at[w])
        start(copy, mine)

    def forward_z(w):
        whole = sets[w][1]
        for d in range(3):
            first[w][d].wait_recv()
            slot = whole.at[(((p["zh"] + 3 - d) % 4) * 2 + core) * 4 + role]
            for k, target in enumerate((xup, xdown, yup if d < 2 else ydown)):
                start(remote(slot, slot, (ps, pr), (w, d * 3 + k), target), second[w])
            start(remote(slot, slot, (cs, cr), (w, d * 4 + 3), sibling), pair[w])

    def forward_xy(w):
        whole = sets[w][1]
        for d in range(3):
            source = (((p["zh"] + 3 - d) % 4) * 2 + core) * 4
            for k, step in ((0, 3), (1, 1), (2, 2)):
                second[w][d * 3 + k].wait_recv()
                slot = whole.at[source + (role + step) % 4]
                start(remote(slot, slot, (cs, cr), (w, d * 4 + k), sibling), pair[w])

    def arrive(w):
        mine[w].wait()
        for copy in pair[w]:
            copy.wait_recv()

    halos = []
    launch_weight(0)
    start(remote(cap, hcap.at[1], (hs, hr), 0, rows[1]), halos)
    start(remote(cap, hcap.at[2], (hs, hr), 1, rows[2]), halos)
    start(remote(cap, hcap.at[0], (hs, hr), 2, rows[0]), halos)
    start(remote(cap, hcap.at[3], (hs, hr), 3, rows[3]), halos)
    launch_weight(1)
    forward_z(0)
    start(remote(grad, hgrad.at[0], (hs, hr), 4, rows[1]), halos)
    start(remote(grad, hgrad.at[1], (hs, hr), 5, rows[2]), halos)
    forward_xy(0)
    forward_z(1)

    def live(v, r):
        return jnp.where((tile + r >= 0) & (tile + r < TILES), v, jnp.zeros_like(v))

    arrive(0)
    for copy in halos[:4]:
        copy.wait_recv()
    x5[0] = live(hcap[0], -2)
    x5[1] = live(hcap[1], -1)
    x5[2] = cap[...]
    x5[3] = live(hcap[2], 1)
    x5[4] = live(hcap[3], 2)
    wide1 = all1[...].reshape(256, 1152)
    for r in range(3):
        for a in range(3):
            xcat[:, a * 128 : (a + 1) * 128] = x5[r + a]
        v = joined(*[dot_nt(xcat[...], wide1[:, b * 384 : (b + 1) * 384]) for b in range(3)])
        if r == 1:
            pre[...] = v
        h = (v * jax.nn.sigmoid(v)).astype(BF16)
        hcat[:, r * 256 : (r + 1) * 256] = h if r == 1 else live(h, r - 1)

    forward_xy(1)

    def one_hot(size, source):
        i = lax.broadcasted_iota(jnp.int32, (size, size), 0)
        j = lax.broadcasted_iota(jnp.int32, (size, size), 1)
        return source(i, j).astype(F32).astype(BF16)

    order_o = one_hot(256, lambda i, j: i == (((j & 127) >> 5) << 6) + ((((j >> 7) + core) & 1) << 5) + (j & 31))
    order_c2 = one_hot(256, lambda i, j: j == (((i >> 3) & 7) << 5) + (((i >> 2) & 1) << 4) + ((i >> 6) << 2) + (i & 3))
    order_c1 = one_hot(128, lambda i, j: j == ((i >> 4) << 4) + (((i >> 1) & 1) << 3) + (((i >> 2) & 3) << 1) + (i & 1))

    def terms(cot, rows_of, order_c, keep, give, block):
        g = dot(cot, order_o)
        shifted = jnp.concatenate([moved(g, -1), g, moved(g, 1)], axis=1).astype(BF16)
        for a in range(3):
            left = dot_nt(order_c, rows_of(a)).astype(BF16)
            t = dot(left, shifted)
            for b in range(3):
                for n in range(t.shape[0] // block):
                    part = t[n * block : (n + 1) * block, b * 256 : (b + 1) * 256]
                    keep[n, a * 3 + b] = part[:, :128]
                    give[n, a * 3 + b] = part[:, 128:].astype(BF16)

    terms(grad[...], lambda a: hcat[:, a * 256 : (a + 1) * 256], order_c2, keep2, give2, 64)
    swap2 = []
    for d in range(4):
        to = (x + d + 1) % 4
        start(remote(give2.at[to], rc2.at[to], (es, er), d, sibling), swap2)

    arrive(1)
    for copy in halos[4:6]:
        copy.wait_recv()
    gcat[0] = live(hgrad[0], -1)
    gcat[1] = grad[...]
    gcat[2] = live(hgrad[1], 1)
    wide2 = all2[...].reshape(256, 2304)
    sums = []
    for b in range(3):
        total = None
        for a in range(3):
            at = ((2 - b) * 3 + (2 - a)) * 256
            part = dot(gcat[a], wide2[:, at : at + 256])
            total = part if total is None else total + part
        sums.append(total)
    v = pre[...]
    sig = jax.nn.sigmoid(v)
    pg[...] = (joined(*sums) * sig * (1.0 + v * (1.0 - sig))).astype(BF16)

    sent2 = []
    for d in range(3):
        to = (x + d + 1) % 4
        swap2[d].wait_recv()
        s2[to] = (keep2[to] + rc2[to].astype(F32)).astype(BF16)
        start(remote(s2.at[to], r2a.at[d], (as_, ar), d, xpeers[d]), sent2)
    start(remote(pg, hpre.at[0], (hs, hr), 6, rows[1]), halos)
    start(remote(pg, hpre.at[1], (hs, hr), 7, rows[2]), halos)

    terms(pg[...], lambda a: x5[a + 1], order_c1, keep1, give1, 16)
    swap1 = []
    start(remote(give1, rc1, (es, er), 4, sibling), swap1)
    cap_out[...] = joined(*[dot_nt(hcat[...], wide2[:, b * 768 : (b + 1) * 768]) for b in range(3)]).astype(BF16)

    swap1[0].wait_recv()
    sent1 = []
    for d in range(7):
        to = (y + d + 1) % 8
        s1[to] = (keep1[to] + rc1[to].astype(F32)).astype(BF16)
        start(remote(s1.at[to], r1a.at[d], (as_, ar), 3 + d, ypeers[d]), sent1)

    swap2[3].wait_recv()
    total = keep2[x] + rc2[x].astype(F32)
    for d in range(3):
        sent2[d].wait_recv()
        total = total + r2a[d].astype(F32)
    for n in range(8):
        k2[n] = total[:, n * 8 : (n + 1) * 8]
        s2b[n] = k2[n].astype(BF16)
    next2 = []
    for d in range(7):
        start(remote(s2b.at[(y + d + 1) % 8], r2b.at[d], (bs, br), d, ypeers[d]), next2)

    total = keep1[y] + rc1[y].astype(F32)
    for d in range(7):
        sent1[d].wait_recv()
        total = total + r1a[d].astype(F32)
    for n in range(4):
        k1[n] = total[:, n * 4 : (n + 1) * 4]
        s1b[n] = k1[n].astype(BF16)
    next1 = []
    for d in range(3):
        start(remote(s1b.at[(x + d + 1) % 4], r1b.at[d], (bs, br), 7 + d, xpeers[d]), next1)

    for copy in halos[6:8]:
        copy.wait_recv()
    three = [live(hpre[0], -1), pg[...], live(hpre[1], 1)]
    sums = []
    for b in range(3):
        total = None
        for a in range(3):
            at = ((2 - b) * 3 + (2 - a)) * 128
            part = dot(three[a], wide1[:, at : at + 128])
            total = part if total is None else total + part
        sums.append(total)
    in_grad[...] = joined(*sums).astype(BF16)

    t2 = k2[y]
    for d in range(7):
        next2[d].wait_recv()
        t2 = t2 + r2b[d].astype(F32)
    t1 = k1[x]
    for d in range(3):
        next1[d].wait_recv()
        t1 = t1 + r1b[d].astype(F32)
    for n in range(2):
        kc[n, :, 0:4] = t2[:, n * 4 : (n + 1) * 4]
        kc[n, :, 4:6] = t1[:, n * 2 : (n + 1) * 2]
        kc[n, :, 6:8] = jnp.zeros((9, 2, 128), F32)
        sc[n] = kc[n].astype(BF16)
    last = []
    for d in range(7):
        start(remote(sc.at[zto[d] % 2], rcz.at[d], (fs, fr), d, zpeers[d]), last)
    total = kc[p["zl"]]
    for d in range(7):
        last[d].wait_recv()
        total = total + rcz[d].astype(F32)
    result[...] = total * SCALE
    for group in first + second + pair + [halos, swap2, swap1, sent2, sent1, next2, next1, last]:
        for copy in group:
            copy.wait_send()


def fused(cap, grad, w1, w2):
    vmem = pl.BlockSpec(memory_space=pltpu.VMEM)
    dma = pltpu.SemaphoreType.DMA
    scratch = [
        ((4, 8, 1152), BF16), ((4, 8, 2304), BF16), ((32, 8, 1152), BF16), ((32, 8, 2304), BF16),
        ((4, 256, 128), BF16), ((2, 256, 256), BF16), ((2, 256, 256), BF16),
        ((5, 256, 128), BF16), ((256, 384), BF16), ((256, 768), BF16), ((3, 256, 256), BF16),
        ((256, 256), F32), ((256, 256), BF16),
        ((8, 9, 16, 128), F32), ((4, 9, 64, 128), F32), ((8, 9, 16, 128), BF16), ((4, 9, 64, 128), BF16),
        ((8, 9, 16, 128), BF16), ((4, 9, 64, 128), BF16), ((8, 9, 16, 128), BF16), ((4, 9, 64, 128), BF16),
        ((7, 9, 16, 128), BF16), ((3, 9, 64, 128), BF16),
        ((4, 9, 4, 128), F32), ((8, 9, 8, 128), F32), ((4, 9, 4, 128), BF16), ((8, 9, 8, 128), BF16),
        ((3, 9, 4, 128), BF16), ((7, 9, 8, 128), BF16),
        ((2, 9, 8, 128), F32), ((2, 9, 8, 128), BF16), ((7, 9, 8, 128), BF16),
    ]
    sems = [(2,)]
    for shape in ((8,), (2, 3), (2, 9), (2, 13), (5,), (10,), (10,), (7,)):
        sems += [shape, shape]
    return pl.pallas_call(
        fused_kernel,
        out_shape=(
            jax.ShapeDtypeStruct((256, 256), BF16),
            jax.ShapeDtypeStruct((256, 128), BF16),
            jax.ShapeDtypeStruct((9, 8, 128), F32),
        ),
        in_specs=[vmem] * 4,
        out_specs=(vmem,) * 3,
        scratch_shapes=[pltpu.VMEM(shape, kind) for shape, kind in scratch] + [dma(shape) for shape in sems],
        compiler_params=pltpu.CompilerParams(
            collective_id=0, has_side_effects=True, vmem_limit_bytes=VMEM_BYTES
        ),
        name="fused",
    )(cap, grad, w1, w2)


def body(cap_in, conv1_weight, conv2_weight, out_grad):
    zh = lax.axis_index("fsdp") // 2
    cap_out, in_grad, result = fused(
        cap_in.reshape(256, 128), out_grad.reshape(256, 256),
        conv1_weight.reshape(1152, 32), conv2_weight.reshape(2304, 32),
    )
    part = lax.dynamic_slice_in_dim(result, zh * 32, 32, axis=2)
    part = jnp.transpose(part, (2, 0, 1)).reshape(32, 3, 3, 8)
    return (
        cap_out.reshape(1, 1, 256, 256),
        in_grad.reshape(1, 1, 256, 128),
        part[..., 4:6],
        part[..., 0:4],
    )


def solution(mesh):
    placed = (
        P("fsdp", "tile", None, None),
        P(None, None, None, "fsdp"),
        P(None, None, None, "fsdp"),
        P("fsdp", "tile", None, None),
    )
    return jax.shard_map(
        body,
        mesh=mesh,
        in_specs=placed,
        out_specs=(
            P("fsdp", "tile", None, None),
            P("fsdp", "tile", None, None),
            P("fsdp", None, None, "tile"),
            P("fsdp", None, None, "tile"),
        ),
        check_vma=False,
    )
```

```python
import math

import jax
import jax.numpy as jnp
from jax import lax
from jax.experimental import pallas as pl
from jax.experimental.pallas import tpu as pltpu
from jax.sharding import PartitionSpec as P

MESH = pl.DeviceIdType.MESH
F32 = jnp.float32
BF16 = jnp.bfloat16
TILES = 64
VMEM_BYTES = 60 * 1024 * 1024
SCALE = 1.0 / math.sqrt(8 * 64 * 256)


def position():
    tile = lax.axis_index("tile")
    fsdp = lax.axis_index("fsdp")
    return dict(x=tile % 4, zl=(tile // 4) % 2, y=tile // 8, zh=fsdp // 2, core=fsdp % 2, tile=tile, fsdp=fsdp)


def device(p, **moved):
    q = {**p, **moved}
    return ((q["y"] * 2 + q["zl"]) * 4 + q["x"], q["zh"] * 2 + q["core"])


def remote(src, dst, sems, index, target):
    send, recv = sems
    return pltpu.make_async_remote_copy(
        src_ref=src, dst_ref=dst, send_sem=send.at[index], recv_sem=recv.at[index],
        device_id=target, device_id_type=MESH,
    )


def dot(a, b):
    return jnp.dot(a, b, preferred_element_type=F32)


def dot_nt(a, b):
    return lax.dot_general(a, b, (((1,), (1,)), ((), ())), preferred_element_type=F32)


def moved(v, step):
    n = v.shape[0]
    pixel = lax.broadcasted_iota(jnp.int32, v.shape, 0)
    if step == 1:
        return jnp.where(pixel == 0, 0.0, pltpu.roll(v, 1, 0))
    return jnp.where(pixel == n - 1, 0.0, pltpu.roll(v, n - 1, 0))


def joined(first, middle, last):
    return middle + moved(first, 1) + moved(last, -1)


def fused_kernel(cap, grad, w1, w2, cap_out, in_grad, grad1, grad2,
                 shard1, shard2, all1, all2, hcap, hgrad, hpre, x5, xcat, hcat, gcat, pre, pg,
                 keep1, keep2, give1, give2, rc1, rc2, s1, s2, r1a, r2a,
                 k1, k2, s1b, s2b, r1b, r2b, kc, sc, rcz,
                 own, hs, hr, zs, zr, ps, pr, cs, cr, es, er, as_, ar, bs, br, fs, fr):
    p = position()
    tile, fsdp, x, y, core = p["tile"], p["fsdp"], p["x"], p["y"], p["core"]
    role = (x + 2 * y) % 4
    sibling = device(p, core=1 - core)
    xpeers = [device(p, x=(x + d) % 4) for d in range(1, 4)]
    ypeers = [device(p, y=(y + d) % 8) for d in range(1, 8)]
    z = p["zh"] * 2 + p["zl"]
    zto = [(z + d) % 8 for d in range(1, 8)]
    zpeers = [device(p, zh=t // 2, zl=t % 2) for t in zto]
    zsame = [device(p, zh=(p["zh"] + d) % 4) for d in (1, 2, 3)]
    rows = [((tile + d) % TILES, fsdp) for d in (2, 1, TILES - 1, TILES - 2)]
    xup, xdown, yup, ydown = xpeers[0], xpeers[2], ypeers[0], ypeers[6]

    barrier = pltpu.get_barrier_semaphore()
    greeted = [sibling] + xpeers + ypeers + zpeers + rows
    for target in greeted:
        pl.semaphore_signal(barrier, inc=1, device_id=target, device_id_type=MESH)

    for weight, shard, c in ((w1, shard1, 128), (w2, shard2, 256)):
        for a in range(3):
            for b in range(3):
                to = (b * 3 + a) * c
                for q in range(4):
                    shard[q, :, to : to + c] = weight[a, b, q * 8 : (q + 1) * 8, :]

    pl.semaphore_wait(barrier, len(greeted))

    sets = ((shard1, all1), (shard2, all2))
    first, second, pair, mine = [[], []], [[], []], [[], []], []

    def start(copy, group):
        copy.start()
        group.append(copy)

    def launch_weight(w):
        shard, whole = sets[w]
        for d in range(3):
            start(remote(shard.at[role], whole.at[fsdp * 4 + role], (zs, zr), (w, d), zsame[d]), first[w])
        start(remote(shard, whole.at[pl.ds(fsdp * 4, 4)], (cs, cr), (w, 12), sibling), pair[w])
        copy = pltpu.make_async_copy(shard, whole.at[pl.ds(fsdp * 4, 4)], own.at[w])
        start(copy, mine)

    def forward_z(w):
        whole = sets[w][1]
        for d in range(3):
            first[w][d].wait_recv()
            slot = whole.at[(((p["zh"] + 3 - d) % 4) * 2 + core) * 4 + role]
            for k, target in enumerate((xup, xdown, yup if d < 2 else ydown)):
                start(remote(slot, slot, (ps, pr), (w, d * 3 + k), target), second[w])
            start(remote(slot, slot, (cs, cr), (w, d * 4 + 3), sibling), pair[w])

    def forward_xy(w):
        whole = sets[w][1]
        for d in range(3):
            source = (((p["zh"] + 3 - d) % 4) * 2 + core) * 4
            for k, step in ((0, 3), (1, 1), (2, 2)):
                second[w][d * 3 + k].wait_recv()
                slot = whole.at[source + (role + step) % 4]
                start(remote(slot, slot, (cs, cr), (w, d * 4 + k), sibling), pair[w])

    def arrive(w):
        mine[w].wait()
        for copy in pair[w]:
            copy.wait_recv()

    halos = []
    launch_weight(0)
    start(remote(cap, hcap.at[1], (hs, hr), 0, rows[1]), halos)
    start(remote(cap, hcap.at[2], (hs, hr), 1, rows[2]), halos)
    start(remote(cap, hcap.at[0], (hs, hr), 2, rows[0]), halos)
    start(remote(cap, hcap.at[3], (hs, hr), 3, rows[3]), halos)
    launch_weight(1)
    forward_z(0)
    start(remote(grad, hgrad.at[0], (hs, hr), 4, rows[1]), halos)
    start(remote(grad, hgrad.at[1], (hs, hr), 5, rows[2]), halos)
    forward_xy(0)
    forward_z(1)

    def live(v, r):
        return jnp.where((tile + r >= 0) & (tile + r < TILES), v, jnp.zeros_like(v))

    arrive(0)
    for copy in halos[:4]:
        copy.wait_recv()
    x5[0] = live(hcap[0], -2)
    x5[1] = live(hcap[1], -1)
    x5[2] = cap[...]
    x5[3] = live(hcap[2], 1)
    x5[4] = live(hcap[3], 2)
    wide1 = all1[...].reshape(256, 1152)
    for r in range(3):
        for a in range(3):
            xcat[:, a * 128 : (a + 1) * 128] = x5[r + a]
        v = joined(*[dot_nt(xcat[...], wide1[:, b * 384 : (b + 1) * 384]) for b in range(3)])
        if r == 1:
            pre[...] = v
        h = (v * jax.nn.sigmoid(v)).astype(BF16)
        hcat[:, r * 256 : (r + 1) * 256] = h if r == 1 else live(h, r - 1)

    forward_xy(1)

    def one_hot(size, source):
        i = lax.broadcasted_iota(jnp.int32, (size, size), 0)
        j = lax.broadcasted_iota(jnp.int32, (size, size), 1)
        return source(i, j).astype(F32).astype(BF16)

    order_o = one_hot(256, lambda i, j: i == (((j & 127) >> 5) << 6) + ((((j >> 7) + core) & 1) << 5) + (j & 31))
    order_c2 = one_hot(256, lambda i, j: j == (((i >> 3) & 7) << 5) + (((i >> 2) & 1) << 4) + ((i >> 6) << 2) + (i & 3))
    order_c1 = one_hot(128, lambda i, j: j == ((i >> 4) << 4) + (((i >> 1) & 1) << 3) + (((i >> 2) & 3) << 1) + (i & 1))

    def terms(cot, rows_of, order_c, keep, give, block):
        g = dot(cot, order_o)
        shifted = jnp.concatenate([moved(g, -1), g, moved(g, 1)], axis=1).astype(BF16)
        for a in range(3):
            left = dot_nt(order_c, rows_of(a)).astype(BF16)
            t = dot(left, shifted)
            for b in range(3):
                for n in range(t.shape[0] // block):
                    part = t[n * block : (n + 1) * block, b * 256 : (b + 1) * 256]
                    keep[n, a * 3 + b] = part[:, :128]
                    give[n, a * 3 + b] = part[:, 128:].astype(BF16)

    terms(grad[...], lambda a: hcat[:, a * 256 : (a + 1) * 256], order_c2, keep2, give2, 64)
    swap2 = []
    for d in range(4):
        to = (x + d + 1) % 4
        start(remote(give2.at[to], rc2.at[to], (es, er), d, sibling), swap2)

    arrive(1)
    for copy in halos[4:6]:
        copy.wait_recv()
    gcat[0] = live(hgrad[0], -1)
    gcat[1] = grad[...]
    gcat[2] = live(hgrad[1], 1)
    wide2 = all2[...].reshape(256, 2304)
    sums = []
    for b in range(3):
        total = None
        for a in range(3):
            at = ((2 - b) * 3 + (2 - a)) * 256
            part = dot(gcat[a], wide2[:, at : at + 256])
            total = part if total is None else total + part
        sums.append(total)
    v = pre[...]
    sig = jax.nn.sigmoid(v)
    pg[...] = (joined(*sums) * sig * (1.0 + v * (1.0 - sig))).astype(BF16)

    sent2 = []
    for d in range(3):
        to = (x + d + 1) % 4
        swap2[d].wait_recv()
        s2[to] = (keep2[to] + rc2[to].astype(F32)).astype(BF16)
        start(remote(s2.at[to], r2a.at[d], (as_, ar), d, xpeers[d]), sent2)
    start(remote(pg, hpre.at[0], (hs, hr), 6, rows[1]), halos)
    start(remote(pg, hpre.at[1], (hs, hr), 7, rows[2]), halos)

    terms(pg[...], lambda a: x5[a + 1], order_c1, keep1, give1, 16)
    swap1 = []
    start(remote(give1, rc1, (es, er), 4, sibling), swap1)
    cap_out[...] = joined(*[dot_nt(hcat[...], wide2[:, b * 768 : (b + 1) * 768]) for b in range(3)]).astype(BF16)

    swap1[0].wait_recv()
    sent1 = []
    for d in range(7):
        to = (y + d + 1) % 8
        s1[to] = (keep1[to] + rc1[to].astype(F32)).astype(BF16)
        start(remote(s1.at[to], r1a.at[d], (as_, ar), 3 + d, ypeers[d]), sent1)

    swap2[3].wait_recv()
    total = keep2[x] + rc2[x].astype(F32)
    for d in range(3):
        sent2[d].wait_recv()
        total = total + r2a[d].astype(F32)
    for n in range(8):
        k2[n] = total[:, n * 8 : (n + 1) * 8]
        s2b[n] = k2[n].astype(BF16)
    next2 = []
    for d in range(7):
        start(remote(s2b.at[(y + d + 1) % 8], r2b.at[d], (bs, br), d, ypeers[d]), next2)

    total = keep1[y] + rc1[y].astype(F32)
    for d in range(7):
        sent1[d].wait_recv()
        total = total + r1a[d].astype(F32)
    for n in range(4):
        k1[n] = total[:, n * 4 : (n + 1) * 4]
        s1b[n] = k1[n].astype(BF16)
    next1 = []
    for d in range(3):
        start(remote(s1b.at[(x + d + 1) % 4], r1b.at[d], (bs, br), 7 + d, xpeers[d]), next1)

    for copy in halos[6:8]:
        copy.wait_recv()
    three = [live(hpre[0], -1), pg[...], live(hpre[1], 1)]
    sums = []
    for b in range(3):
        total = None
        for a in range(3):
            at = ((2 - b) * 3 + (2 - a)) * 128
            part = dot(three[a], wide1[:, at : at + 128])
            total = part if total is None else total + part
        sums.append(total)
    in_grad[...] = joined(*sums).astype(BF16)

    t2 = k2[y]
    for d in range(7):
        next2[d].wait_recv()
        t2 = t2 + r2b[d].astype(F32)
    t1 = k1[x]
    for d in range(3):
        next1[d].wait_recv()
        t1 = t1 + r1b[d].astype(F32)
    for n in range(2):
        kc[n, :, 0:4] = t2[:, n * 4 : (n + 1) * 4]
        kc[n, :, 4:6] = t1[:, n * 2 : (n + 1) * 2]
        kc[n, :, 6:8] = jnp.zeros((9, 2, 128), F32)
        sc[n] = kc[n].astype(BF16)
    last = []
    for d in range(7):
        start(remote(sc.at[zto[d] % 2], rcz.at[d], (fs, fr), d, zpeers[d]), last)
    total = kc[p["zl"]]
    for d in range(7):
        last[d].wait_recv()
        total = total + rcz[d].astype(F32)
    total = total * SCALE
    mine_o = total[:, :, 0:32]
    for n in range(1, 4):
        mine_o = jnp.where(p["zh"] == n, total[:, :, n * 32 : (n + 1) * 32], mine_o)
    grad2[...] = mine_o[:, 0:4]
    grad1[...] = mine_o[:, 4:6]
    for group in first + second + pair + [halos, swap2, swap1, sent2, sent1, next2, next1, last]:
        for copy in group:
            copy.wait_send()


def fused(cap, grad, w1, w2):
    vmem = pl.BlockSpec(memory_space=pltpu.VMEM)
    dma = pltpu.SemaphoreType.DMA
    scratch = [
        ((4, 8, 1152), BF16), ((4, 8, 2304), BF16), ((32, 8, 1152), BF16), ((32, 8, 2304), BF16),
        ((4, 256, 128), BF16), ((2, 256, 256), BF16), ((2, 256, 256), BF16),
        ((5, 256, 128), BF16), ((256, 384), BF16), ((256, 768), BF16), ((3, 256, 256), BF16),
        ((256, 256), F32), ((256, 256), BF16),
        ((8, 9, 16, 128), F32), ((4, 9, 64, 128), F32), ((8, 9, 16, 128), BF16), ((4, 9, 64, 128), BF16),
        ((8, 9, 16, 128), BF16), ((4, 9, 64, 128), BF16), ((8, 9, 16, 128), BF16), ((4, 9, 64, 128), BF16),
        ((7, 9, 16, 128), BF16), ((3, 9, 64, 128), BF16),
        ((4, 9, 4, 128), F32), ((8, 9, 8, 128), F32), ((4, 9, 4, 128), BF16), ((8, 9, 8, 128), BF16),
        ((3, 9, 4, 128), BF16), ((7, 9, 8, 128), BF16),
        ((2, 9, 8, 128), F32), ((2, 9, 8, 128), BF16), ((7, 9, 8, 128), BF16),
    ]
    sems = [(2,)]
    for shape in ((8,), (2, 3), (2, 9), (2, 13), (5,), (10,), (10,), (7,)):
        sems += [shape, shape]
    return pl.pallas_call(
        fused_kernel,
        out_shape=(
            jax.ShapeDtypeStruct((256, 256), BF16),
            jax.ShapeDtypeStruct((256, 128), BF16),
            jax.ShapeDtypeStruct((9, 2, 32), F32),
            jax.ShapeDtypeStruct((9, 4, 32), F32),
        ),
        in_specs=[vmem] * 4,
        out_specs=(vmem,) * 4,
        scratch_shapes=[pltpu.VMEM(shape, kind) for shape, kind in scratch] + [dma(shape) for shape in sems],
        compiler_params=pltpu.CompilerParams(
            collective_id=0, has_side_effects=True, vmem_limit_bytes=VMEM_BYTES
        ),
        name="fused",
    )(cap, grad, w1, w2)


def hand_over(*arrays):
    def kernel(*refs):
        for source, target in zip(refs[: len(arrays)], refs[len(arrays) :]):
            target[...] = source[...]

    vmem = pl.BlockSpec(memory_space=pltpu.VMEM)
    return pl.pallas_call(
        kernel,
        out_shape=tuple(jax.ShapeDtypeStruct(v.shape, v.dtype) for v in arrays),
        in_specs=[vmem] * len(arrays),
        out_specs=(vmem,) * len(arrays),
        name="hand_over",
    )(*arrays)


def body(cap_in, conv1_weight, conv2_weight, out_grad):
    cap_out, in_grad, grad1, grad2 = fused(
        cap_in.reshape(256, 128), out_grad.reshape(256, 256),
        jnp.transpose(conv1_weight, (0, 1, 3, 2)), jnp.transpose(conv2_weight, (0, 1, 3, 2)),
    )
    cap_out, in_grad, grad1, grad2 = hand_over(cap_out, in_grad, grad1, grad2)
    return (
        cap_out.reshape(1, 1, 256, 256),
        in_grad.reshape(1, 1, 256, 128),
        jnp.transpose(grad1.reshape(3, 3, 2, 32), (3, 0, 1, 2)),
        jnp.transpose(grad2.reshape(3, 3, 4, 32), (3, 0, 1, 2)),
    )


def solution(mesh):
    placed = (
        P("fsdp", "tile", None, None),
        P(None, None, None, "fsdp"),
        P(None, None, None, "fsdp"),
        P("fsdp", "tile", None, None),
    )
    return jax.shard_map(
        body,
        mesh=mesh,
        in_specs=placed,
        out_specs=(
            P("fsdp", "tile", None, None),
            P("fsdp", "tile", None, None),
            P("fsdp", None, None, "tile"),
            P("fsdp", None, None, "tile"),
        ),
        check_vma=False,
    )
```

```python
import math

import jax
import jax.numpy as jnp
from jax import lax
from jax.experimental import pallas as pl
from jax.experimental.pallas import tpu as pltpu
from jax.sharding import PartitionSpec as P

MESH = pl.DeviceIdType.MESH
F32 = jnp.float32
BF16 = jnp.bfloat16
TILES = 64
VMEM_BYTES = 60 * 1024 * 1024
SCALE = 1.0 / math.sqrt(8 * 64 * 256)


def position():
    tile = lax.axis_index("tile")
    fsdp = lax.axis_index("fsdp")
    return dict(x=tile % 4, zl=(tile // 4) % 2, y=tile // 8, zh=fsdp // 2, core=fsdp % 2, tile=tile, fsdp=fsdp)


def device(p, **moved):
    q = {**p, **moved}
    return ((q["y"] * 2 + q["zl"]) * 4 + q["x"], q["zh"] * 2 + q["core"])


def remote(src, dst, sems, index, target):
    send, recv = sems
    return pltpu.make_async_remote_copy(
        src_ref=src, dst_ref=dst, send_sem=send.at[index], recv_sem=recv.at[index],
        device_id=target, device_id_type=MESH,
    )


def dot(a, b):
    return jnp.dot(a, b, preferred_element_type=F32)


def dot_nt(a, b):
    return lax.dot_general(a, b, (((1,), (1,)), ((), ())), preferred_element_type=F32)


def moved(v, step):
    n = v.shape[0]
    pixel = lax.broadcasted_iota(jnp.int32, v.shape, 0)
    if step == 1:
        return jnp.where(pixel == 0, 0.0, pltpu.roll(v, 1, 0))
    return jnp.where(pixel == n - 1, 0.0, pltpu.roll(v, n - 1, 0))


def joined(first, middle, last):
    return middle + moved(first, 1) + moved(last, -1)


def fused_kernel(cap, grad, w1, w2, cap_out, in_grad, grad1, grad2,
                 shard1, shard2, all1, all2, hcap, hgrad, hpre, x5, xcat, hcat, gcat, pre, pg,
                 keep1, keep2, give1, give2, rc1, rc2, s1, s2, r1a, r2a,
                 k1, k2, s1b, s2b, r1b, r2b, kc, kp, sc, rcz,
                 own, hs, hr, zs, zr, ps, pr, cs, cr, es, er, as_, ar, bs, br, fs, fr):
    p = position()
    tile, fsdp, x, y, core = p["tile"], p["fsdp"], p["x"], p["y"], p["core"]
    role = (2 * x + y) % 4
    sibling = device(p, core=1 - core)
    xpeers = [device(p, x=(x + d) % 4) for d in range(1, 4)]
    ypeers = [device(p, y=(y + d) % 8) for d in range(1, 8)]
    z = p["zh"] * 2 + p["zl"]
    zto = [(z + d) % 8 for d in range(1, 8)]
    zpeers = [device(p, zh=t // 2, zl=t % 2) for t in zto]
    zsame = [device(p, zh=(p["zh"] + d) % 4) for d in (1, 2, 3)]
    rows = [((tile + d) % TILES, fsdp) for d in (1, TILES - 1)]
    xup, xdown, yup, ydown = xpeers[0], xpeers[2], ypeers[0], ypeers[6]

    barrier = pltpu.get_barrier_semaphore()
    greeted = [sibling] + xpeers + ypeers + zpeers + rows
    for target in greeted:
        pl.semaphore_signal(barrier, inc=1, device_id=target, device_id_type=MESH)

    for weight, shard, c in ((w1, shard1, 128), (w2, shard2, 256)):
        for a in range(3):
            for b in range(3):
                to = (b * 3 + a) * c
                for q in range(4):
                    shard[q, :, to : to + c] = weight[a, b, q * 8 : (q + 1) * 8, :]

    pl.semaphore_wait(barrier, len(greeted))

    sets = ((shard1, all1), (shard2, all2))
    first, second, pair, mine = [[], []], [[], []], [[], []], []

    def start(copy, group):
        copy.start()
        group.append(copy)

    def launch_weight(w):
        shard, whole = sets[w]
        for d in range(3):
            start(remote(shard.at[role], whole.at[fsdp * 4 + role], (zs, zr), (w, d), zsame[d]), first[w])
        start(remote(shard, whole.at[pl.ds(fsdp * 4, 4)], (cs, cr), (w, 12), sibling), pair[w])
        copy = pltpu.make_async_copy(shard, whole.at[pl.ds(fsdp * 4, 4)], own.at[w])
        start(copy, mine)

    def forward_z(w):
        whole = sets[w][1]
        for d in range(3):
            first[w][d].wait_recv()
            slot = whole.at[(((p["zh"] + 3 - d) % 4) * 2 + core) * 4 + role]
            for k, target in enumerate((yup, ydown, xup if d < 2 else xdown)):
                start(remote(slot, slot, (ps, pr), (w, d * 3 + k), target), second[w])
            start(remote(slot, slot, (cs, cr), (w, d * 4 + 3), sibling), pair[w])

    def forward_xy(w):
        whole = sets[w][1]
        for d in range(3):
            source = (((p["zh"] + 3 - d) % 4) * 2 + core) * 4
            for k, step in ((0, 3), (1, 1), (2, 2)):
                second[w][d * 3 + k].wait_recv()
                slot = whole.at[source + (role + step) % 4]
                start(remote(slot, slot, (cs, cr), (w, d * 4 + k), sibling), pair[w])

    def arrive(w):
        mine[w].wait()
        for copy in pair[w]:
            copy.wait_recv()

    halos = []
    launch_weight(0)
    start(remote(cap, hcap.at[1], (hs, hr), 0, rows[0]), halos)
    start(remote(cap, hcap.at[2], (hs, hr), 1, rows[1]), halos)
    launch_weight(1)
    forward_z(0)
    for d in range(2):
        halos[d].wait_recv()
        start(remote(hcap.at[1 + d], hcap.at[3 * d], (hs, hr), 2 + d, rows[d]), halos)
    forward_xy(0)
    start(remote(grad, hgrad.at[0], (hs, hr), 4, rows[0]), halos)
    start(remote(grad, hgrad.at[1], (hs, hr), 5, rows[1]), halos)
    forward_z(1)

    def live(v, r):
        return jnp.where((tile + r >= 0) & (tile + r < TILES), v, jnp.zeros_like(v))

    arrive(0)
    for copy in halos[2:4]:
        copy.wait_recv()
    x5[0] = live(hcap[0], -2)
    x5[1] = live(hcap[1], -1)
    x5[2] = cap[...]
    x5[3] = live(hcap[2], 1)
    x5[4] = live(hcap[3], 2)
    wide1 = all1[...].reshape(256, 1152)
    for r in range(3):
        for a in range(3):
            xcat[:, a * 128 : (a + 1) * 128] = x5[r + a]
        v = joined(*[dot_nt(xcat[...], wide1[:, b * 384 : (b + 1) * 384]) for b in range(3)])
        if r == 1:
            pre[...] = v
        h = (v * jax.nn.sigmoid(v)).astype(BF16)
        hcat[:, r * 256 : (r + 1) * 256] = h if r == 1 else live(h, r - 1)

    forward_xy(1)

    def one_hot(size, source):
        i = lax.broadcasted_iota(jnp.int32, (size, size), 0)
        j = lax.broadcasted_iota(jnp.int32, (size, size), 1)
        return source(i, j).astype(F32).astype(BF16)

    order_o = one_hot(256, lambda i, j: i == (((j & 127) >> 5) << 6) + ((((j >> 7) + core) & 1) << 5) + (j & 31))
    order_c2 = one_hot(256, lambda i, j: j == (((i >> 3) & 7) << 5) + (((i >> 2) & 1) << 4) + ((i >> 6) << 2) + (i & 3))
    order_c1 = one_hot(128, lambda i, j: j == (((i >> 2) & 7) << 4) + (((i >> 1) & 1) << 3) + ((i >> 5) << 1) + (i & 1))

    def terms(cot, rows_of, order_c, keep, give, block):
        g = dot(cot, order_o)
        shifted = jnp.concatenate([moved(g, -1), g, moved(g, 1)], axis=1).astype(BF16)
        for a in range(3):
            left = dot_nt(order_c, rows_of(a)).astype(BF16)
            t = dot(left, shifted)
            for b in range(3):
                for n in range(t.shape[0] // block):
                    part = t[n * block : (n + 1) * block, b * 256 : (b + 1) * 256]
                    keep[n, a * 3 + b] = part[:, :128]
                    give[n, a * 3 + b] = part[:, 128:].astype(BF16)

    terms(grad[...], lambda a: hcat[:, a * 256 : (a + 1) * 256], order_c2, keep2, give2, 64)
    swap2 = []
    for d in range(4):
        to = (x + d + 1) % 4
        start(remote(give2.at[to], rc2.at[to], (es, er), d, sibling), swap2)

    sent2 = []
    for d in range(3):
        to = (x + d + 1) % 4
        swap2[d].wait_recv()
        s2[to] = (keep2[to] + rc2[to].astype(F32)).astype(BF16)
        start(remote(s2.at[to], r2a.at[d], (as_, ar), d, xpeers[d]), sent2)

    arrive(1)
    for copy in halos[4:6]:
        copy.wait_recv()
    gcat[0] = live(hgrad[0], -1)
    gcat[1] = grad[...]
    gcat[2] = live(hgrad[1], 1)
    wide2 = all2[...].reshape(256, 2304)
    sums = []
    for b in range(3):
        total = None
        for a in range(3):
            at = ((2 - b) * 3 + (2 - a)) * 256
            part = dot(gcat[a], wide2[:, at : at + 256])
            total = part if total is None else total + part
        sums.append(total)
    v = pre[...]
    sig = jax.nn.sigmoid(v)
    pg[...] = (joined(*sums) * sig * (1.0 + v * (1.0 - sig))).astype(BF16)

    terms(pg[...], lambda a: x5[a + 1], order_c1, keep1, give1, 32)
    swap1 = []
    start(remote(give1, rc1, (es, er), 4, sibling), swap1)
    cap_out[...] = joined(*[dot_nt(hcat[...], wide2[:, b * 768 : (b + 1) * 768]) for b in range(3)]).astype(BF16)

    swap1[0].wait_recv()
    sent1 = []
    for d in range(3):
        to = (x + d + 1) % 4
        s1[to] = (keep1[to] + rc1[to].astype(F32)).astype(BF16)
        start(remote(s1.at[to], r1a.at[d], (as_, ar), 3 + d, xpeers[d]), sent1)
    start(remote(pg, hpre.at[0], (hs, hr), 6, rows[0]), halos)
    start(remote(pg, hpre.at[1], (hs, hr), 7, rows[1]), halos)

    swap2[3].wait_recv()
    total = keep2[x] + rc2[x].astype(F32)
    for d in range(3):
        sent2[d].wait_recv()
        total = total + r2a[d].astype(F32)
    for n in range(8):
        k2[n] = total[:, n * 8 : (n + 1) * 8]
        s2b[n] = k2[n].astype(BF16)
    next2 = []
    for d in range(7):
        start(remote(s2b.at[(y + d + 1) % 8], r2b.at[d], (bs, br), d, ypeers[d]), next2)

    total = keep1[x] + rc1[x].astype(F32)
    for d in range(3):
        sent1[d].wait_recv()
        total = total + r1a[d].astype(F32)
    for n in range(8):
        k1[n] = total[:, n * 4 : (n + 1) * 4]
        s1b[n] = k1[n].astype(BF16)
    next1 = []
    for d in range(7):
        start(remote(s1b.at[(y + d + 1) % 8], r1b.at[d], (bs, br), 7 + d, ypeers[d]), next1)

    for copy in halos[6:8]:
        copy.wait_recv()
    three = [live(hpre[0], -1), pg[...], live(hpre[1], 1)]
    sums = []
    for b in range(3):
        total = None
        for a in range(3):
            at = ((2 - b) * 3 + (2 - a)) * 128
            part = dot(three[a], wide1[:, at : at + 128])
            total = part if total is None else total + part
        sums.append(total)
    in_grad[...] = joined(*sums).astype(BF16)

    t2 = k2[y]
    for d in range(7):
        next2[d].wait_recv()
        t2 = t2 + r2b[d].astype(F32)
    t1 = k1[y]
    for d in range(7):
        next1[d].wait_recv()
        t1 = t1 + r1b[d].astype(F32)
    quarter = lax.broadcasted_iota(jnp.int32, (8, 128), 1) >> 5
    for n in range(2):
        kc[n, :, 0:4] = t2[:, n * 4 : (n + 1) * 4]
        kc[n, :, 4:6] = t1[:, n * 2 : (n + 1) * 2]
        kc[n, :, 6:8] = jnp.zeros((9, 2, 128), F32)
        turned = [
            [kc[n, tap] if turn == 0 else pltpu.roll(kc[n, tap], turn * 32, 1) for turn in range(4)]
            for tap in range(9)
        ]
        for h in range(4):
            for g in range(3):
                packed = turned[g * 4][(4 - h) % 4]
                for k in range(1, 4 if g < 2 else 1):
                    packed = jnp.where(quarter == k, turned[g * 4 + k][(k - h) % 4], packed)
                kp[n, h, g] = packed
            sc[n, h] = kp[n, h].astype(BF16)
    last = []
    for d in range(7):
        start(remote(sc.at[zto[d] % 2, zto[d] // 2], rcz.at[d], (fs, fr), d, zpeers[d]), last)
    total = kp[p["zl"], p["zh"]]
    for d in range(7):
        last[d].wait_recv()
        total = total + rcz[d].astype(F32)
    total = total * SCALE
    for tap in range(9):
        mine_o = total[tap // 4, :, (tap % 4) * 32 : (tap % 4 + 1) * 32]
        grad2[tap] = mine_o[0:4]
        grad1[tap] = mine_o[4:6]
    for group in first + second + pair + [halos, swap2, swap1, sent2, sent1, next2, next1, last]:
        for copy in group:
            copy.wait_send()


def fused(cap, grad, w1, w2):
    vmem = pl.BlockSpec(memory_space=pltpu.VMEM)
    dma = pltpu.SemaphoreType.DMA
    scratch = [
        ((4, 8, 1152), BF16), ((4, 8, 2304), BF16), ((32, 8, 1152), BF16), ((32, 8, 2304), BF16),
        ((4, 256, 128), BF16), ((2, 256, 256), BF16), ((2, 256, 256), BF16),
        ((5, 256, 128), BF16), ((256, 384), BF16), ((256, 768), BF16), ((3, 256, 256), BF16),
        ((256, 256), F32), ((256, 256), BF16),
        ((4, 9, 32, 128), F32), ((4, 9, 64, 128), F32), ((4, 9, 32, 128), BF16), ((4, 9, 64, 128), BF16),
        ((4, 9, 32, 128), BF16), ((4, 9, 64, 128), BF16), ((4, 9, 32, 128), BF16), ((4, 9, 64, 128), BF16),
        ((3, 9, 32, 128), BF16), ((3, 9, 64, 128), BF16),
        ((8, 9, 4, 128), F32), ((8, 9, 8, 128), F32), ((8, 9, 4, 128), BF16), ((8, 9, 8, 128), BF16),
        ((7, 9, 4, 128), BF16), ((7, 9, 8, 128), BF16),
        ((2, 9, 8, 128), F32), ((2, 4, 3, 8, 128), F32), ((2, 4, 3, 8, 128), BF16), ((7, 3, 8, 128), BF16),
    ]
    sems = [(2,)]
    for shape in ((8,), (2, 3), (2, 9), (2, 13), (5,), (6,), (14,), (7,)):
        sems += [shape, shape]
    return pl.pallas_call(
        fused_kernel,
        out_shape=(
            jax.ShapeDtypeStruct((256, 256), BF16),
            jax.ShapeDtypeStruct((256, 128), BF16),
            jax.ShapeDtypeStruct((9, 2, 32), F32),
            jax.ShapeDtypeStruct((9, 4, 32), F32),
        ),
        in_specs=[vmem] * 4,
        out_specs=(vmem,) * 4,
        scratch_shapes=[pltpu.VMEM(shape, kind) for shape, kind in scratch] + [dma(shape) for shape in sems],
        compiler_params=pltpu.CompilerParams(
            collective_id=0, has_side_effects=True, vmem_limit_bytes=VMEM_BYTES
        ),
        name="fused",
    )(cap, grad, w1, w2)


def hand_over(*arrays):
    def kernel(*refs):
        for source, target in zip(refs[: len(arrays)], refs[len(arrays) :]):
            target[...] = source[...]

    vmem = pl.BlockSpec(memory_space=pltpu.VMEM)
    return pl.pallas_call(
        kernel,
        out_shape=tuple(jax.ShapeDtypeStruct(v.shape, v.dtype) for v in arrays),
        in_specs=[vmem] * len(arrays),
        out_specs=(vmem,) * len(arrays),
        name="hand_over",
    )(*arrays)


def body(cap_in, conv1_weight, conv2_weight, out_grad):
    cap_out, in_grad, grad1, grad2 = fused(
        cap_in.reshape(256, 128), out_grad.reshape(256, 256),
        jnp.transpose(conv1_weight, (0, 1, 3, 2)), jnp.transpose(conv2_weight, (0, 1, 3, 2)),
    )
    cap_out, in_grad, grad1, grad2 = hand_over(cap_out, in_grad, grad1, grad2)
    return (
        cap_out.reshape(1, 1, 256, 256),
        in_grad.reshape(1, 1, 256, 128),
        jnp.transpose(grad1.reshape(3, 3, 2, 32), (3, 0, 1, 2)),
        jnp.transpose(grad2.reshape(3, 3, 4, 32), (3, 0, 1, 2)),
    )


def solution(mesh):
    placed = (
        P("fsdp", "tile", None, None),
        P(None, None, None, "fsdp"),
        P(None, None, None, "fsdp"),
        P("fsdp", "tile", None, None),
    )
    return jax.shard_map(
        body,
        mesh=mesh,
        in_specs=placed,
        out_specs=(
            P("fsdp", "tile", None, None),
            P("fsdp", "tile", None, None),
            P("fsdp", None, None, "tile"),
            P("fsdp", None, None, "tile"),
        ),
        check_vma=False,
    )
```

```python
import math

import jax
import jax.numpy as jnp
from jax import lax
from jax.experimental import pallas as pl
from jax.experimental.pallas import tpu as pltpu
from jax.sharding import PartitionSpec as P

MESH = pl.DeviceIdType.MESH
F32 = jnp.float32
BF16 = jnp.bfloat16
TILES = 64
VMEM_BYTES = 60 * 1024 * 1024
SCALE = 1.0 / math.sqrt(8 * 64 * 256)


def position():
    tile = lax.axis_index("tile")
    fsdp = lax.axis_index("fsdp")
    return dict(x=tile % 4, zl=(tile // 4) % 2, y=tile // 8, zh=fsdp // 2, core=fsdp % 2, tile=tile, fsdp=fsdp)


def device(p, **moved):
    q = {**p, **moved}
    return ((q["y"] * 2 + q["zl"]) * 4 + q["x"], q["zh"] * 2 + q["core"])


def remote(src, dst, sems, index, target):
    send, recv = sems
    return pltpu.make_async_remote_copy(
        src_ref=src, dst_ref=dst, send_sem=send.at[index], recv_sem=recv.at[index],
        device_id=target, device_id_type=MESH,
    )


def dot(a, b):
    return jnp.dot(a, b, preferred_element_type=F32)


def dot_nt(a, b):
    return lax.dot_general(a, b, (((1,), (1,)), ((), ())), preferred_element_type=F32)


def moved(v, step):
    n = v.shape[0]
    pixel = lax.broadcasted_iota(jnp.int32, v.shape, 0)
    if step == 1:
        return jnp.where(pixel == 0, 0.0, pltpu.roll(v, 1, 0))
    return jnp.where(pixel == n - 1, 0.0, pltpu.roll(v, n - 1, 0))


def joined(first, middle, last):
    return middle + moved(first, 1) + moved(last, -1)


def fused_kernel(cap, grad, w1, w2, cap_out, in_grad, grad1, grad2,
                 shard1, shard2, all1, all2, hcap, hgrad, hpre, x5, xcat, hcat, gcat, pre, pg,
                 keep1, keep2, give1, give2, rc1, rc2, s1, s2, r1a, r2a,
                 k1, k2, s1b, s2b, r1b, r2b, kc, kp, sc, rcz,
                 own, hs, hr, zs, zr, ps, pr, cs, cr, es, er, as_, ar, bs, br, fs, fr):
    p = position()
    tile, fsdp, x, y, core = p["tile"], p["fsdp"], p["x"], p["y"], p["core"]
    role = (2 * x + y) % 4
    sibling = device(p, core=1 - core)
    xpeers = [device(p, x=(x + d) % 4) for d in range(1, 4)]
    ypeers = [device(p, y=(y + d) % 8) for d in range(1, 8)]
    z = p["zh"] * 2 + p["zl"]
    zto = [(z + d) % 8 for d in range(1, 8)]
    zpeers = [device(p, zh=t // 2, zl=t % 2) for t in zto]
    zsame = [device(p, zh=(p["zh"] + d) % 4) for d in (1, 2, 3)]
    rows = [((tile + d) % TILES, fsdp) for d in (1, TILES - 1)]
    xup, xdown, yup, ydown = xpeers[0], xpeers[2], ypeers[0], ypeers[6]

    barrier = pltpu.get_barrier_semaphore()
    greeted = [sibling] + xpeers + ypeers + zpeers + rows
    for target in greeted:
        pl.semaphore_signal(barrier, inc=1, device_id=target, device_id_type=MESH)

    for weight, shard, c in ((w1, shard1, 128), (w2, shard2, 256)):
        for a in range(3):
            for b in range(3):
                to = (b * 3 + a) * c
                for q in range(4):
                    shard[q, :, to : to + c] = weight[a, b, q * 8 : (q + 1) * 8, :]

    pl.semaphore_wait(barrier, len(greeted))

    sets = ((shard1, all1), (shard2, all2))
    first, second, pair, mine = [[], []], [[], []], [[], []], []

    def start(copy, group):
        copy.start()
        group.append(copy)

    def launch_weight(w):
        shard, whole = sets[w]
        for d in range(3):
            start(remote(shard.at[role], whole.at[fsdp * 4 + role], (zs, zr), (w, d), zsame[d]), first[w])
        start(remote(shard, whole.at[pl.ds(fsdp * 4, 4)], (cs, cr), (w, 12), sibling), pair[w])
        copy = pltpu.make_async_copy(shard, whole.at[pl.ds(fsdp * 4, 4)], own.at[w])
        start(copy, mine)

    def forward_z(w):
        whole = sets[w][1]
        for d in range(3):
            first[w][d].wait_recv()
            slot = whole.at[(((p["zh"] + 3 - d) % 4) * 2 + core) * 4 + role]
            for k, target in enumerate((yup, ydown, xup if d < 2 else xdown)):
                start(remote(slot, slot, (ps, pr), (w, d * 3 + k), target), second[w])
            start(remote(slot, slot, (cs, cr), (w, d * 4 + 3), sibling), pair[w])

    def forward_xy(w):
        whole = sets[w][1]
        for d in range(3):
            source = (((p["zh"] + 3 - d) % 4) * 2 + core) * 4
            for k, step in ((0, 3), (1, 1), (2, 2)):
                second[w][d * 3 + k].wait_recv()
                slot = whole.at[source + (role + step) % 4]
                start(remote(slot, slot, (cs, cr), (w, d * 4 + k), sibling), pair[w])

    def arrive(w):
        mine[w].wait()
        for copy in pair[w]:
            copy.wait_recv()

    halos = []
    launch_weight(0)
    start(remote(cap, hcap.at[1], (hs, hr), 0, rows[0]), halos)
    start(remote(cap, hcap.at[2], (hs, hr), 1, rows[1]), halos)
    forward_z(0)
    launch_weight(1)
    for d in range(2):
        halos[d].wait_recv()
        start(remote(hcap.at[1 + d], hcap.at[3 * d], (hs, hr), 2 + d, rows[d]), halos)
    forward_xy(0)
    start(remote(grad, hgrad.at[0], (hs, hr), 4, rows[0]), halos)
    start(remote(grad, hgrad.at[1], (hs, hr), 5, rows[1]), halos)

    def live(v, r):
        return jnp.where((tile + r >= 0) & (tile + r < TILES), v, jnp.zeros_like(v))

    arrive(0)
    for copy in halos[2:4]:
        copy.wait_recv()
    x5[0] = live(hcap[0], -2)
    x5[1] = live(hcap[1], -1)
    x5[2] = cap[...]
    x5[3] = live(hcap[2], 1)
    x5[4] = live(hcap[3], 2)
    wide1 = all1[...].reshape(256, 1152)
    for r in range(3):
        for a in range(3):
            xcat[:, a * 128 : (a + 1) * 128] = x5[r + a]
        v = joined(*[dot_nt(xcat[...], wide1[:, b * 384 : (b + 1) * 384]) for b in range(3)])
        if r == 1:
            pre[...] = v
        h = (v * jax.nn.sigmoid(v)).astype(BF16)
        hcat[:, r * 256 : (r + 1) * 256] = h if r == 1 else live(h, r - 1)

    forward_z(1)

    def one_hot(size, source):
        i = lax.broadcasted_iota(jnp.int32, (size, size), 0)
        j = lax.broadcasted_iota(jnp.int32, (size, size), 1)
        return source(i, j).astype(F32).astype(BF16)

    order_o = one_hot(256, lambda i, j: i == (((j & 127) >> 5) << 6) + ((((j >> 7) + core) & 1) << 5) + (j & 31))
    order_c2 = one_hot(256, lambda i, j: j == (((i >> 3) & 7) << 5) + (((i >> 2) & 1) << 4) + ((i >> 6) << 2) + (i & 3))
    order_c1 = one_hot(128, lambda i, j: j == (((i >> 2) & 7) << 4) + (((i >> 1) & 1) << 3) + ((i >> 5) << 1) + (i & 1))

    def terms(cot, rows_of, order_c, keep, give, block):
        g = dot(cot, order_o)
        shifted = jnp.concatenate([moved(g, -1), g, moved(g, 1)], axis=1).astype(BF16)
        for a in range(3):
            left = dot_nt(order_c, rows_of(a)).astype(BF16)
            t = dot(left, shifted)
            for b in range(3):
                for n in range(t.shape[0] // block):
                    part = t[n * block : (n + 1) * block, b * 256 : (b + 1) * 256]
                    keep[n, a * 3 + b] = part[:, :128]
                    give[n, a * 3 + b] = part[:, 128:].astype(BF16)

    terms(grad[...], lambda a: hcat[:, a * 256 : (a + 1) * 256], order_c2, keep2, give2, 64)
    swap2 = []
    for d in range(4):
        to = (x + d + 1) % 4
        start(remote(give2.at[to], rc2.at[to], (es, er), d, sibling), swap2)

    sent2 = []
    for d in range(3):
        to = (x + d + 1) % 4
        swap2[d].wait_recv()
        s2[to] = (keep2[to] + rc2[to].astype(F32)).astype(BF16)
        start(remote(s2.at[to], r2a.at[d], (as_, ar), d, xpeers[d]), sent2)

    forward_xy(1)

    arrive(1)
    for copy in halos[4:6]:
        copy.wait_recv()
    gcat[0] = live(hgrad[0], -1)
    gcat[1] = grad[...]
    gcat[2] = live(hgrad[1], 1)
    wide2 = all2[...].reshape(256, 2304)
    sums = []
    for b in range(3):
        total = None
        for a in range(3):
            at = ((2 - b) * 3 + (2 - a)) * 256
            part = dot(gcat[a], wide2[:, at : at + 256])
            total = part if total is None else total + part
        sums.append(total)
    v = pre[...]
    sig = jax.nn.sigmoid(v)
    pg[...] = (joined(*sums) * sig * (1.0 + v * (1.0 - sig))).astype(BF16)

    terms(pg[...], lambda a: x5[a + 1], order_c1, keep1, give1, 32)
    swap1 = []
    start(remote(give1, rc1, (es, er), 4, sibling), swap1)
    swap2[3].wait_recv()
    total = keep2[x] + rc2[x].astype(F32)
    for d in range(3):
        sent2[d].wait_recv()
        total = total + r2a[d].astype(F32)
    for n in range(8):
        k2[n] = total[:, n * 8 : (n + 1) * 8]
        s2b[n] = k2[n].astype(BF16)
    next2 = []
    for d in range(7):
        start(remote(s2b.at[(y + d + 1) % 8], r2b.at[d], (bs, br), d, ypeers[d]), next2)

    swap1[0].wait_recv()
    sent1 = []
    for d in range(3):
        to = (x + d + 1) % 4
        s1[to] = (keep1[to] + rc1[to].astype(F32)).astype(BF16)
        start(remote(s1.at[to], r1a.at[d], (as_, ar), 3 + d, xpeers[d]), sent1)
    start(remote(pg, hpre.at[0], (hs, hr), 6, rows[0]), halos)
    start(remote(pg, hpre.at[1], (hs, hr), 7, rows[1]), halos)

    cap_out[...] = joined(*[dot_nt(hcat[...], wide2[:, b * 768 : (b + 1) * 768]) for b in range(3)]).astype(BF16)

    total = keep1[x] + rc1[x].astype(F32)
    for d in range(3):
        sent1[d].wait_recv()
        total = total + r1a[d].astype(F32)
    for n in range(8):
        k1[n] = total[:, n * 4 : (n + 1) * 4]
        s1b[n] = k1[n].astype(BF16)
    next1 = []
    for d in range(7):
        start(remote(s1b.at[(y + d + 1) % 8], r1b.at[d], (bs, br), 7 + d, ypeers[d]), next1)

    for copy in halos[6:8]:
        copy.wait_recv()
    three = [live(hpre[0], -1), pg[...], live(hpre[1], 1)]
    sums = []
    for b in range(3):
        total = None
        for a in range(3):
            at = ((2 - b) * 3 + (2 - a)) * 128
            part = dot(three[a], wide1[:, at : at + 128])
            total = part if total is None else total + part
        sums.append(total)
    in_grad[...] = joined(*sums).astype(BF16)

    t2 = k2[y]
    for d in range(7):
        next2[d].wait_recv()
        t2 = t2 + r2b[d].astype(F32)
    t1 = k1[y]
    for d in range(7):
        next1[d].wait_recv()
        t1 = t1 + r1b[d].astype(F32)
    quarter = lax.broadcasted_iota(jnp.int32, (8, 128), 1) >> 5
    for n in range(2):
        kc[n, :, 0:4] = t2[:, n * 4 : (n + 1) * 4]
        kc[n, :, 4:6] = t1[:, n * 2 : (n + 1) * 2]
        kc[n, :, 6:8] = jnp.zeros((9, 2, 128), F32)
        turned = [
            [kc[n, tap] if turn == 0 else pltpu.roll(kc[n, tap], turn * 32, 1) for turn in range(4)]
            for tap in range(9)
        ]
        for h in range(4):
            for g in range(3):
                packed = turned[g * 4][(4 - h) % 4]
                for k in range(1, 4 if g < 2 else 1):
                    packed = jnp.where(quarter == k, turned[g * 4 + k][(k - h) % 4], packed)
                kp[n, h, g] = packed
            sc[n, h] = kp[n, h].astype(BF16)
    last = []
    for d in range(7):
        start(remote(sc.at[zto[d] % 2, zto[d] // 2], rcz.at[d], (fs, fr), d, zpeers[d]), last)
    total = kp[p["zl"], p["zh"]]
    for d in range(7):
        last[d].wait_recv()
        total = total + rcz[d].astype(F32)
    total = total * SCALE
    for tap in range(9):
        mine_o = total[tap // 4, :, (tap % 4) * 32 : (tap % 4 + 1) * 32]
        grad2[tap] = mine_o[0:4]
        grad1[tap] = mine_o[4:6]
    for group in first + second + pair + [halos, swap2, swap1, sent2, sent1, next2, next1, last]:
        for copy in group:
            copy.wait_send()


def fused(cap, grad, w1, w2):
    vmem = pl.BlockSpec(memory_space=pltpu.VMEM)
    dma = pltpu.SemaphoreType.DMA
    scratch = [
        ((4, 8, 1152), BF16), ((4, 8, 2304), BF16), ((32, 8, 1152), BF16), ((32, 8, 2304), BF16),
        ((4, 256, 128), BF16), ((2, 256, 256), BF16), ((2, 256, 256), BF16),
        ((5, 256, 128), BF16), ((256, 384), BF16), ((256, 768), BF16), ((3, 256, 256), BF16),
        ((256, 256), F32), ((256, 256), BF16),
        ((4, 9, 32, 128), F32), ((4, 9, 64, 128), F32), ((4, 9, 32, 128), BF16), ((4, 9, 64, 128), BF16),
        ((4, 9, 32, 128), BF16), ((4, 9, 64, 128), BF16), ((4, 9, 32, 128), BF16), ((4, 9, 64, 128), BF16),
        ((3, 9, 32, 128), BF16), ((3, 9, 64, 128), BF16),
        ((8, 9, 4, 128), F32), ((8, 9, 8, 128), F32), ((8, 9, 4, 128), BF16), ((8, 9, 8, 128), BF16),
        ((7, 9, 4, 128), BF16), ((7, 9, 8, 128), BF16),
        ((2, 9, 8, 128), F32), ((2, 4, 3, 8, 128), F32), ((2, 4, 3, 8, 128), BF16), ((7, 3, 8, 128), BF16),
    ]
    sems = [(2,)]
    for shape in ((8,), (2, 3), (2, 9), (2, 13), (5,), (6,), (14,), (7,)):
        sems += [shape, shape]
    return pl.pallas_call(
        fused_kernel,
        out_shape=(
            jax.ShapeDtypeStruct((256, 256), BF16),
            jax.ShapeDtypeStruct((256, 128), BF16),
            jax.ShapeDtypeStruct((9, 2, 32), F32),
            jax.ShapeDtypeStruct((9, 4, 32), F32),
        ),
        in_specs=[vmem] * 4,
        out_specs=(vmem,) * 4,
        scratch_shapes=[pltpu.VMEM(shape, kind) for shape, kind in scratch] + [dma(shape) for shape in sems],
        compiler_params=pltpu.CompilerParams(
            collective_id=0, has_side_effects=True, vmem_limit_bytes=VMEM_BYTES
        ),
        name="fused",
    )(cap, grad, w1, w2)


def hand_over(*arrays):
    def kernel(*refs):
        for source, target in zip(refs[: len(arrays)], refs[len(arrays) :]):
            target[...] = source[...]

    vmem = pl.BlockSpec(memory_space=pltpu.VMEM)
    return pl.pallas_call(
        kernel,
        out_shape=tuple(jax.ShapeDtypeStruct(v.shape, v.dtype) for v in arrays),
        in_specs=[vmem] * len(arrays),
        out_specs=(vmem,) * len(arrays),
        name="hand_over",
    )(*arrays)


def body(cap_in, conv1_weight, conv2_weight, out_grad):
    cap_out, in_grad, grad1, grad2 = fused(
        cap_in.reshape(256, 128), out_grad.reshape(256, 256),
        jnp.transpose(conv1_weight, (0, 1, 3, 2)), jnp.transpose(conv2_weight, (0, 1, 3, 2)),
    )
    cap_out, in_grad, grad1, grad2 = hand_over(cap_out, in_grad, grad1, grad2)
    return (
        cap_out.reshape(1, 1, 256, 256),
        in_grad.reshape(1, 1, 256, 128),
        jnp.transpose(grad1.reshape(3, 3, 2, 32), (3, 0, 1, 2)),
        jnp.transpose(grad2.reshape(3, 3, 4, 32), (3, 0, 1, 2)),
    )


def solution(mesh):
    placed = (
        P("fsdp", "tile", None, None),
        P(None, None, None, "fsdp"),
        P(None, None, None, "fsdp"),
        P("fsdp", "tile", None, None),
    )
    return jax.shard_map(
        body,
        mesh=mesh,
        in_specs=placed,
        out_specs=(
            P("fsdp", "tile", None, None),
            P("fsdp", "tile", None, None),
            P("fsdp", None, None, "tile"),
            P("fsdp", None, None, "tile"),
        ),
        check_vma=False,
    )
```

```python
import math

import jax
import jax.numpy as jnp
from jax import lax
from jax.experimental import pallas as pl
from jax.experimental.pallas import tpu as pltpu
from jax.sharding import PartitionSpec as P

MESH = pl.DeviceIdType.MESH
F32 = jnp.float32
BF16 = jnp.bfloat16
TILES = 64
FAR4 = (1, 0, 2)
FAR8 = (3, 2, 4, 1, 5, 0, 6)
VMEM_BYTES = 60 * 1024 * 1024
SCALE = 1.0 / math.sqrt(8 * 64 * 256)


def position():
    tile = lax.axis_index("tile")
    fsdp = lax.axis_index("fsdp")
    return dict(x=tile % 4, zl=(tile // 4) % 2, y=tile // 8, zh=fsdp // 2, core=fsdp % 2, tile=tile, fsdp=fsdp)


def device(p, **moved):
    q = {**p, **moved}
    return ((q["y"] * 2 + q["zl"]) * 4 + q["x"], q["zh"] * 2 + q["core"])


def remote(src, dst, sems, index, target):
    send, recv = sems
    return pltpu.make_async_remote_copy(
        src_ref=src, dst_ref=dst, send_sem=send.at[index], recv_sem=recv.at[index],
        device_id=target, device_id_type=MESH,
    )


def dot(a, b):
    return jnp.dot(a, b, preferred_element_type=F32)


def dot_nt(a, b):
    return lax.dot_general(a, b, (((1,), (1,)), ((), ())), preferred_element_type=F32)


def moved(v, step):
    n = v.shape[0]
    pixel = lax.broadcasted_iota(jnp.int32, v.shape, 0)
    if step == 1:
        return jnp.where(pixel == 0, 0.0, pltpu.roll(v, 1, 0))
    return jnp.where(pixel == n - 1, 0.0, pltpu.roll(v, n - 1, 0))


def joined(first, middle, last):
    return middle + moved(first, 1) + moved(last, -1)


def fused_kernel(cap, grad, w1, w2, cap_out, in_grad, grad1, grad2,
                 shard1, shard2, all1, all2, hcap, hgrad, hpre, x5, xcat, hcat, gcat, pre, pg,
                 keep1, keep2, give1, give2, rc1, rc2, s1, s2, r1a, r2a,
                 k1, k2, s1b, s2b, r1b, r2b, kc, kp, sc, rcz,
                 own, hs, hr, zs, zr, ps, pr, cs, cr, es, er, as_, ar, bs, br, fs, fr):
    p = position()
    tile, fsdp, x, y, core = p["tile"], p["fsdp"], p["x"], p["y"], p["core"]
    role = (2 * x + y) % 4
    sibling = device(p, core=1 - core)
    xpeers = [device(p, x=(x + d) % 4) for d in range(1, 4)]
    ypeers = [device(p, y=(y + d) % 8) for d in range(1, 8)]
    z = p["zh"] * 2 + p["zl"]
    zto = [(z + d) % 8 for d in range(1, 8)]
    zpeers = [device(p, zh=t // 2, zl=t % 2) for t in zto]
    zsame = [device(p, zh=(p["zh"] + d) % 4) for d in (1, 2, 3)]
    rows = [((tile + d) % TILES, fsdp) for d in (1, TILES - 1)]
    xup, xdown, yup, ydown = xpeers[0], xpeers[2], ypeers[0], ypeers[6]

    barrier = pltpu.get_barrier_semaphore()
    greeted = [sibling] + xpeers + ypeers + zpeers + rows
    for target in greeted:
        pl.semaphore_signal(barrier, inc=1, device_id=target, device_id_type=MESH)

    for weight, shard, c in ((w1, shard1, 128), (w2, shard2, 256)):
        for a in range(3):
            for b in range(3):
                to = (b * 3 + a) * c
                for q in range(4):
                    shard[q, :, to : to + c] = weight[a, b, q * 8 : (q + 1) * 8, :]

    pl.semaphore_wait(barrier, len(greeted))

    sets = ((shard1, all1), (shard2, all2))
    first, second, pair, mine = [{}, {}], [[], []], [[], []], []

    def start(copy, group):
        copy.start()
        group.append(copy)

    def start_at(copy, group, d):
        copy.start()
        group[d] = copy

    def launch_weight(w):
        shard, whole = sets[w]
        for d in FAR4:
            start_at(remote(shard.at[role], whole.at[fsdp * 4 + role], (zs, zr), (w, d), zsame[d]), first[w], d)
        start(remote(shard, whole.at[pl.ds(fsdp * 4, 4)], (cs, cr), (w, 12), sibling), pair[w])
        copy = pltpu.make_async_copy(shard, whole.at[pl.ds(fsdp * 4, 4)], own.at[w])
        start(copy, mine)

    def forward_z(w):
        whole = sets[w][1]
        for d in range(3):
            first[w][d].wait_recv()
            slot = whole.at[(((p["zh"] + 3 - d) % 4) * 2 + core) * 4 + role]
            for k, target in enumerate((yup, ydown, xup if d < 2 else xdown)):
                start(remote(slot, slot, (ps, pr), (w, d * 3 + k), target), second[w])
            start(remote(slot, slot, (cs, cr), (w, d * 4 + 3), sibling), pair[w])

    def forward_xy(w):
        whole = sets[w][1]
        for d in range(3):
            source = (((p["zh"] + 3 - d) % 4) * 2 + core) * 4
            for k, step in ((0, 3), (1, 1), (2, 2)):
                second[w][d * 3 + k].wait_recv()
                slot = whole.at[source + (role + step) % 4]
                start(remote(slot, slot, (cs, cr), (w, d * 4 + k), sibling), pair[w])

    def arrive(w):
        mine[w].wait()
        for copy in pair[w]:
            copy.wait_recv()

    halos = []
    launch_weight(0)
    start(remote(cap, hcap.at[1], (hs, hr), 0, rows[0]), halos)
    start(remote(cap, hcap.at[2], (hs, hr), 1, rows[1]), halos)
    forward_z(0)
    launch_weight(1)
    for d in range(2):
        halos[d].wait_recv()
        start(remote(hcap.at[1 + d], hcap.at[3 * d], (hs, hr), 2 + d, rows[d]), halos)
    forward_xy(0)
    start(remote(grad, hgrad.at[0], (hs, hr), 4, rows[0]), halos)
    start(remote(grad, hgrad.at[1], (hs, hr), 5, rows[1]), halos)

    def live(v, r):
        return jnp.where((tile + r >= 0) & (tile + r < TILES), v, jnp.zeros_like(v))

    arrive(0)
    for copy in halos[2:4]:
        copy.wait_recv()
    x5[0] = live(hcap[0], -2)
    x5[1] = live(hcap[1], -1)
    x5[2] = cap[...]
    x5[3] = live(hcap[2], 1)
    x5[4] = live(hcap[3], 2)
    wide1 = all1[...].reshape(256, 1152)
    for r in range(3):
        for a in range(3):
            xcat[:, a * 128 : (a + 1) * 128] = x5[r + a]
        v = joined(*[dot_nt(xcat[...], wide1[:, b * 384 : (b + 1) * 384]) for b in range(3)])
        if r == 1:
            pre[...] = v
        h = (v * jax.nn.sigmoid(v)).astype(BF16)
        hcat[:, r * 256 : (r + 1) * 256] = h if r == 1 else live(h, r - 1)

    forward_z(1)

    def one_hot(size, source):
        i = lax.broadcasted_iota(jnp.int32, (size, size), 0)
        j = lax.broadcasted_iota(jnp.int32, (size, size), 1)
        return source(i, j).astype(F32).astype(BF16)

    order_o = one_hot(256, lambda i, j: i == (((j & 127) >> 5) << 6) + ((((j >> 7) + core) & 1) << 5) + (j & 31))
    order_c2 = one_hot(256, lambda i, j: j == (((i >> 3) & 7) << 5) + (((i >> 2) & 1) << 4) + ((i >> 6) << 2) + (i & 3))
    order_c1 = one_hot(128, lambda i, j: j == (((i >> 2) & 7) << 4) + (((i >> 1) & 1) << 3) + ((i >> 5) << 1) + (i & 1))

    def terms(cot, rows_of, order_c, keep, give, block):
        g = dot(cot, order_o)
        shifted = jnp.concatenate([moved(g, -1), g, moved(g, 1)], axis=1).astype(BF16)
        for a in range(3):
            left = dot_nt(order_c, rows_of(a)).astype(BF16)
            t = dot(left, shifted)
            for b in range(3):
                for n in range(t.shape[0] // block):
                    part = t[n * block : (n + 1) * block, b * 256 : (b + 1) * 256]
                    keep[n, a * 3 + b] = part[:, :128]
                    give[n, a * 3 + b] = part[:, 128:].astype(BF16)

    terms(grad[...], lambda a: hcat[:, a * 256 : (a + 1) * 256], order_c2, keep2, give2, 64)
    swap2 = {}
    for d in FAR4 + (3,):
        to = (x + d + 1) % 4
        start_at(remote(give2.at[to], rc2.at[to], (es, er), d, sibling), swap2, d)

    sent2 = {}
    for d in FAR4:
        to = (x + d + 1) % 4
        swap2[d].wait_recv()
        s2[to] = (keep2[to] + rc2[to].astype(F32)).astype(BF16)
        start_at(remote(s2.at[to], r2a.at[d], (as_, ar), d, xpeers[d]), sent2, d)

    forward_xy(1)

    arrive(1)
    for copy in halos[4:6]:
        copy.wait_recv()
    gcat[0] = live(hgrad[0], -1)
    gcat[1] = grad[...]
    gcat[2] = live(hgrad[1], 1)
    wide2 = all2[...].reshape(256, 2304)
    sums = []
    for b in range(3):
        total = None
        for a in range(3):
            at = ((2 - b) * 3 + (2 - a)) * 256
            part = dot(gcat[a], wide2[:, at : at + 256])
            total = part if total is None else total + part
        sums.append(total)
    v = pre[...]
    sig = jax.nn.sigmoid(v)
    pg[...] = (joined(*sums) * sig * (1.0 + v * (1.0 - sig))).astype(BF16)

    terms(pg[...], lambda a: x5[a + 1], order_c1, keep1, give1, 32)
    swap1 = []
    start(remote(give1, rc1, (es, er), 4, sibling), swap1)
    swap2[3].wait_recv()
    total = keep2[x] + rc2[x].astype(F32)
    for d in range(3):
        sent2[d].wait_recv()
        total = total + r2a[d].astype(F32)
    for n in range(8):
        k2[n] = total[:, n * 8 : (n + 1) * 8]
        s2b[n] = k2[n].astype(BF16)
    next2 = {}
    for d in FAR8:
        start_at(remote(s2b.at[(y + d + 1) % 8], r2b.at[d], (bs, br), d, ypeers[d]), next2, d)

    swap1[0].wait_recv()
    sent1 = {}
    for d in FAR4:
        to = (x + d + 1) % 4
        s1[to] = (keep1[to] + rc1[to].astype(F32)).astype(BF16)
        start_at(remote(s1.at[to], r1a.at[d], (as_, ar), 3 + d, xpeers[d]), sent1, d)
    start(remote(pg, hpre.at[0], (hs, hr), 6, rows[0]), halos)
    start(remote(pg, hpre.at[1], (hs, hr), 7, rows[1]), halos)

    cap_out[...] = joined(*[dot_nt(hcat[...], wide2[:, b * 768 : (b + 1) * 768]) for b in range(3)]).astype(BF16)

    total = keep1[x] + rc1[x].astype(F32)
    for d in range(3):
        sent1[d].wait_recv()
        total = total + r1a[d].astype(F32)
    for n in range(8):
        k1[n] = total[:, n * 4 : (n + 1) * 4]
        s1b[n] = k1[n].astype(BF16)
    next1 = {}
    for d in FAR8:
        start_at(remote(s1b.at[(y + d + 1) % 8], r1b.at[d], (bs, br), 7 + d, ypeers[d]), next1, d)

    for copy in halos[6:8]:
        copy.wait_recv()
    three = [live(hpre[0], -1), pg[...], live(hpre[1], 1)]
    sums = []
    for b in range(3):
        total = None
        for a in range(3):
            at = ((2 - b) * 3 + (2 - a)) * 128
            part = dot(three[a], wide1[:, at : at + 128])
            total = part if total is None else total + part
        sums.append(total)
    in_grad[...] = joined(*sums).astype(BF16)

    t2 = k2[y]
    for d in range(7):
        next2[d].wait_recv()
        t2 = t2 + r2b[d].astype(F32)
    t1 = k1[y]
    for d in range(7):
        next1[d].wait_recv()
        t1 = t1 + r1b[d].astype(F32)
    quarter = lax.broadcasted_iota(jnp.int32, (8, 128), 1) >> 5
    for n in range(2):
        kc[n, :, 0:4] = t2[:, n * 4 : (n + 1) * 4]
        kc[n, :, 4:6] = t1[:, n * 2 : (n + 1) * 2]
        kc[n, :, 6:8] = jnp.zeros((9, 2, 128), F32)
        turned = [
            [kc[n, tap] if turn == 0 else pltpu.roll(kc[n, tap], turn * 32, 1) for turn in range(4)]
            for tap in range(9)
        ]
        for h in range(4):
            for g in range(3):
                packed = turned[g * 4][(4 - h) % 4]
                for k in range(1, 4 if g < 2 else 1):
                    packed = jnp.where(quarter == k, turned[g * 4 + k][(k - h) % 4], packed)
                kp[n, h, g] = packed
            sc[n, h] = kp[n, h].astype(BF16)
    last = {}
    for d in FAR8:
        start_at(remote(sc.at[zto[d] % 2, zto[d] // 2], rcz.at[d], (fs, fr), d, zpeers[d]), last, d)
    total = kp[p["zl"], p["zh"]]
    for d in range(7):
        last[d].wait_recv()
        total = total + rcz[d].astype(F32)
    total = total * SCALE
    for tap in range(9):
        mine_o = total[tap // 4, :, (tap % 4) * 32 : (tap % 4 + 1) * 32]
        grad2[tap] = mine_o[0:4]
        grad1[tap] = mine_o[4:6]
    for group in first + second + pair + [halos, swap2, swap1, sent2, sent1, next2, next1, last]:
        for copy in group.values() if isinstance(group, dict) else group:
            copy.wait_send()


def fused(cap, grad, w1, w2):
    vmem = pl.BlockSpec(memory_space=pltpu.VMEM)
    dma = pltpu.SemaphoreType.DMA
    scratch = [
        ((4, 8, 1152), BF16), ((4, 8, 2304), BF16), ((32, 8, 1152), BF16), ((32, 8, 2304), BF16),
        ((4, 256, 128), BF16), ((2, 256, 256), BF16), ((2, 256, 256), BF16),
        ((5, 256, 128), BF16), ((256, 384), BF16), ((256, 768), BF16), ((3, 256, 256), BF16),
        ((256, 256), F32), ((256, 256), BF16),
        ((4, 9, 32, 128), F32), ((4, 9, 64, 128), F32), ((4, 9, 32, 128), BF16), ((4, 9, 64, 128), BF16),
        ((4, 9, 32, 128), BF16), ((4, 9, 64, 128), BF16), ((4, 9, 32, 128), BF16), ((4, 9, 64, 128), BF16),
        ((3, 9, 32, 128), BF16), ((3, 9, 64, 128), BF16),
        ((8, 9, 4, 128), F32), ((8, 9, 8, 128), F32), ((8, 9, 4, 128), BF16), ((8, 9, 8, 128), BF16),
        ((7, 9, 4, 128), BF16), ((7, 9, 8, 128), BF16),
        ((2, 9, 8, 128), F32), ((2, 4, 3, 8, 128), F32), ((2, 4, 3, 8, 128), BF16), ((7, 3, 8, 128), BF16),
    ]
    sems = [(2,)]
    for shape in ((8,), (2, 3), (2, 9), (2, 13), (5,), (6,), (14,), (7,)):
        sems += [shape, shape]
    return pl.pallas_call(
        fused_kernel,
        out_shape=(
            jax.ShapeDtypeStruct((256, 256), BF16),
            jax.ShapeDtypeStruct((256, 128), BF16),
            jax.ShapeDtypeStruct((9, 2, 32), F32),
            jax.ShapeDtypeStruct((9, 4, 32), F32),
        ),
        in_specs=[vmem] * 4,
        out_specs=(vmem,) * 4,
        scratch_shapes=[pltpu.VMEM(shape, kind) for shape, kind in scratch] + [dma(shape) for shape in sems],
        compiler_params=pltpu.CompilerParams(
            collective_id=0, has_side_effects=True, vmem_limit_bytes=VMEM_BYTES
        ),
        name="fused",
    )(cap, grad, w1, w2)


def hand_over(*arrays):
    def kernel(*refs):
        for source, target in zip(refs[: len(arrays)], refs[len(arrays) :]):
            target[...] = source[...]

    vmem = pl.BlockSpec(memory_space=pltpu.VMEM)
    return pl.pallas_call(
        kernel,
        out_shape=tuple(jax.ShapeDtypeStruct(v.shape, v.dtype) for v in arrays),
        in_specs=[vmem] * len(arrays),
        out_specs=(vmem,) * len(arrays),
        name="hand_over",
    )(*arrays)


def body(cap_in, conv1_weight, conv2_weight, out_grad):
    cap_out, in_grad, grad1, grad2 = fused(
        cap_in.reshape(256, 128), out_grad.reshape(256, 256),
        jnp.transpose(conv1_weight, (0, 1, 3, 2)), jnp.transpose(conv2_weight, (0, 1, 3, 2)),
    )
    cap_out, in_grad, grad1, grad2 = hand_over(cap_out, in_grad, grad1, grad2)
    return (
        cap_out.reshape(1, 1, 256, 256),
        in_grad.reshape(1, 1, 256, 128),
        jnp.transpose(grad1.reshape(3, 3, 2, 32), (3, 0, 1, 2)),
        jnp.transpose(grad2.reshape(3, 3, 4, 32), (3, 0, 1, 2)),
    )


def solution(mesh):
    placed = (
        P("fsdp", "tile", None, None),
        P(None, None, None, "fsdp"),
        P(None, None, None, "fsdp"),
        P("fsdp", "tile", None, None),
    )
    return jax.shard_map(
        body,
        mesh=mesh,
        in_specs=placed,
        out_specs=(
            P("fsdp", "tile", None, None),
            P("fsdp", "tile", None, None),
            P("fsdp", None, None, "tile"),
            P("fsdp", None, None, "tile"),
        ),
        check_vma=False,
    )
```

```python
import math

import jax
import jax.numpy as jnp
from jax import lax
from jax.experimental import pallas as pl
from jax.experimental.pallas import tpu as pltpu
from jax.sharding import PartitionSpec as P

MESH = pl.DeviceIdType.MESH
F32 = jnp.float32
BF16 = jnp.bfloat16
TILES = 64
FAR4 = (1, 0, 2)
FAR8 = (3, 2, 4, 1, 5, 0, 6)
VMEM_BYTES = 60 * 1024 * 1024
SCALE = 1.0 / math.sqrt(8 * 64 * 256)


def position():
    tile = lax.axis_index("tile")
    fsdp = lax.axis_index("fsdp")
    return dict(x=tile % 4, zl=(tile // 4) % 2, y=tile // 8, zh=fsdp // 2, core=fsdp % 2, tile=tile, fsdp=fsdp)


def device(p, **moved):
    q = {**p, **moved}
    return ((q["y"] * 2 + q["zl"]) * 4 + q["x"], q["zh"] * 2 + q["core"])


def remote(src, dst, sems, index, target):
    send, recv = sems
    return pltpu.make_async_remote_copy(
        src_ref=src, dst_ref=dst, send_sem=send.at[index], recv_sem=recv.at[index],
        device_id=target, device_id_type=MESH,
    )


def dot(a, b):
    return jnp.dot(a, b, preferred_element_type=F32)


def dot_nt(a, b):
    return lax.dot_general(a, b, (((1,), (1,)), ((), ())), preferred_element_type=F32)


def moved(v, step):
    n = v.shape[0]
    pixel = lax.broadcasted_iota(jnp.int32, v.shape, 0)
    if step == 1:
        return jnp.where(pixel == 0, 0.0, pltpu.roll(v, 1, 0))
    return jnp.where(pixel == n - 1, 0.0, pltpu.roll(v, n - 1, 0))


def joined(first, middle, last):
    return middle + moved(first, 1) + moved(last, -1)


def fused_kernel(cap, grad, w1, w2, cap_out, in_grad, grad1, grad2,
                 shard1, shard2, all1, all2, hcap, hgrad, hpre, x5, xcat, hcat, gcat, pre, pg,
                 keep1, keep2, give1, give2, rc1, rc2, s1, s2, r1a, r2a,
                 k1, k2, s1b, s2b, r1b, r2b, kc, kp, sc, rcz,
                 own, hs, hr, zs, zr, ps, pr, cs, cr, es, er, as_, ar, bs, br, fs, fr):
    p = position()
    tile, fsdp, x, y, core = p["tile"], p["fsdp"], p["x"], p["y"], p["core"]
    role = (2 * x + y) % 4
    sibling = device(p, core=1 - core)
    xpeers = [device(p, x=(x + d) % 4) for d in range(1, 4)]
    ypeers = [device(p, y=(y + d) % 8) for d in range(1, 8)]
    z = p["zh"] * 2 + p["zl"]
    zto = [(z + d) % 8 for d in range(1, 8)]
    zpeers = [device(p, zh=t // 2, zl=t % 2) for t in zto]
    zsame = [device(p, zh=(p["zh"] + d) % 4) for d in (1, 2, 3)]
    rows = [((tile + d) % TILES, fsdp) for d in (1, TILES - 1)]
    xup, xdown, yup, ydown = xpeers[0], xpeers[2], ypeers[0], ypeers[6]

    barrier = pltpu.get_barrier_semaphore()
    greeted = [sibling] + xpeers + ypeers + zpeers + rows
    for target in greeted:
        pl.semaphore_signal(barrier, inc=1, device_id=target, device_id_type=MESH)

    for weight, shard, c in ((w1, shard1, 128), (w2, shard2, 256)):
        for a in range(3):
            for b in range(3):
                to = (b * 3 + a) * c
                for q in range(4):
                    shard[q, :, to : to + c] = weight[a, b, q * 8 : (q + 1) * 8, :]

    pl.semaphore_wait(barrier, len(greeted))

    sets = ((shard1, all1), (shard2, all2))
    first, second, pair, mine = [{}, {}], [[], []], [[], []], []

    def start(copy, group):
        copy.start()
        group.append(copy)

    def start_at(copy, group, d):
        copy.start()
        group[d] = copy

    def launch_weight(w):
        shard, whole = sets[w]
        for d in FAR4:
            start_at(remote(shard.at[role], whole.at[fsdp * 4 + role], (zs, zr), (w, d), zsame[d]), first[w], d)
        start(remote(shard, whole.at[pl.ds(fsdp * 4, 4)], (cs, cr), (w, 12), sibling), pair[w])
        copy = pltpu.make_async_copy(shard, whole.at[pl.ds(fsdp * 4, 4)], own.at[w])
        start(copy, mine)

    def forward_z(w):
        whole = sets[w][1]
        for d in range(3):
            first[w][d].wait_recv()
            slot = whole.at[(((p["zh"] + 3 - d) % 4) * 2 + core) * 4 + role]
            for k, target in enumerate((yup, ydown, xup if d < 2 else xdown)):
                start(remote(slot, slot, (ps, pr), (w, d * 3 + k), target), second[w])
            start(remote(slot, slot, (cs, cr), (w, d * 4 + 3), sibling), pair[w])

    def forward_xy(w):
        whole = sets[w][1]
        for d in range(3):
            source = (((p["zh"] + 3 - d) % 4) * 2 + core) * 4
            for k, step in ((0, 3), (1, 1), (2, 2)):
                second[w][d * 3 + k].wait_recv()
                slot = whole.at[source + (role + step) % 4]
                start(remote(slot, slot, (cs, cr), (w, d * 4 + k), sibling), pair[w])

    def arrive(w):
        mine[w].wait()
        for copy in pair[w]:
            copy.wait_recv()

    halos = []
    launch_weight(0)
    start(remote(cap, hcap.at[1], (hs, hr), 0, rows[0]), halos)
    start(remote(cap, hcap.at[2], (hs, hr), 1, rows[1]), halos)
    forward_z(0)
    launch_weight(1)
    for d in range(2):
        halos[d].wait_recv()
        start(remote(hcap.at[1 + d], hcap.at[3 * d], (hs, hr), 2 + d, rows[d]), halos)
    forward_xy(0)
    start(remote(grad, hgrad.at[0], (hs, hr), 4, rows[0]), halos)
    start(remote(grad, hgrad.at[1], (hs, hr), 5, rows[1]), halos)

    def live(v, r):
        return jnp.where((tile + r >= 0) & (tile + r < TILES), v, jnp.zeros_like(v))

    arrive(0)
    for copy in halos[2:4]:
        copy.wait_recv()
    x5[0] = live(hcap[0], -2)
    x5[1] = live(hcap[1], -1)
    x5[2] = cap[...]
    x5[3] = live(hcap[2], 1)
    x5[4] = live(hcap[3], 2)
    wide1 = all1[...].reshape(256, 1152)
    for r in range(3):
        for a in range(3):
            xcat[:, a * 128 : (a + 1) * 128] = x5[r + a]
        v = joined(*[dot_nt(xcat[...], wide1[:, b * 384 : (b + 1) * 384]) for b in range(3)])
        if r == 1:
            pre[...] = v
        h = (v * jax.nn.sigmoid(v)).astype(BF16)
        hcat[:, r * 256 : (r + 1) * 256] = h if r == 1 else live(h, r - 1)

    forward_z(1)

    def one_hot(size, source):
        i = lax.broadcasted_iota(jnp.int32, (size, size), 0)
        j = lax.broadcasted_iota(jnp.int32, (size, size), 1)
        return source(i, j).astype(F32).astype(BF16)

    order_o = one_hot(256, lambda i, j: i == (((j & 127) >> 5) << 6) + ((((j >> 7) + core) & 1) << 5) + (j & 31))
    order_c2 = one_hot(256, lambda i, j: j == (((i >> 3) & 7) << 5) + (((i >> 2) & 1) << 4) + ((i >> 6) << 2) + (i & 3))
    order_c1 = one_hot(128, lambda i, j: j == (((i >> 2) & 7) << 4) + (((i >> 1) & 1) << 3) + ((i >> 5) << 1) + (i & 1))

    def terms(cot, rows_of, order_c, keep, give, block):
        g = dot(cot, order_o)
        shifted = jnp.concatenate([moved(g, -1), g, moved(g, 1)], axis=1).astype(BF16)
        for a in range(3):
            left = dot_nt(order_c, rows_of(a)).astype(BF16)
            t = dot(left, shifted)
            for b in range(3):
                for n in range(t.shape[0] // block):
                    part = t[n * block : (n + 1) * block, b * 256 : (b + 1) * 256]
                    keep[n, a * 3 + b] = part[:, :128]
                    give[n, a * 3 + b] = part[:, 128:].astype(BF16)

    terms(grad[...], lambda a: hcat[:, a * 256 : (a + 1) * 256], order_c2, keep2, give2, 64)
    swap2 = {}
    for d in FAR4 + (3,):
        to = (x + d + 1) % 4
        start_at(remote(give2.at[to], rc2.at[to], (es, er), d, sibling), swap2, d)

    sent2 = {}
    for d in FAR4:
        to = (x + d + 1) % 4
        swap2[d].wait_recv()
        s2[to] = (keep2[to] + rc2[to].astype(F32)).astype(BF16)
        start_at(remote(s2.at[to], r2a.at[d], (as_, ar), d, xpeers[d]), sent2, d)

    forward_xy(1)

    arrive(1)
    for copy in halos[4:6]:
        copy.wait_recv()
    gcat[0] = live(hgrad[0], -1)
    gcat[1] = grad[...]
    gcat[2] = live(hgrad[1], 1)
    wide2 = all2[...].reshape(256, 2304)
    sums = []
    for b in range(3):
        total = None
        for a in range(3):
            at = ((2 - b) * 3 + (2 - a)) * 256
            part = dot(gcat[a], wide2[:, at : at + 256])
            total = part if total is None else total + part
        sums.append(total)
    v = pre[...]
    sig = jax.nn.sigmoid(v)
    pg[...] = (joined(*sums) * sig * (1.0 + v * (1.0 - sig))).astype(BF16)

    terms(pg[...], lambda a: x5[a + 1], order_c1, keep1, give1, 32)
    swap1 = {}
    for d in FAR4 + (3,):
        to = (x + d + 1) % 4
        start_at(remote(give1.at[to], rc1.at[to], (es, er), 4 + d, sibling), swap1, d)
    swap2[3].wait_recv()
    total = keep2[x] + rc2[x].astype(F32)
    for d in range(3):
        sent2[d].wait_recv()
        total = total + r2a[d].astype(F32)
    for n in range(8):
        k2[n] = total[:, n * 8 : (n + 1) * 8]
        s2b[n] = k2[n].astype(BF16)
    next2 = {}
    for d in FAR8:
        start_at(remote(s2b.at[(y + d + 1) % 8], r2b.at[d], (bs, br), d, ypeers[d]), next2, d)

    sent1 = {}
    for d in FAR4:
        to = (x + d + 1) % 4
        swap1[d].wait_recv()
        s1[to] = (keep1[to] + rc1[to].astype(F32)).astype(BF16)
        start_at(remote(s1.at[to], r1a.at[d], (as_, ar), 3 + d, xpeers[d]), sent1, d)
    start(remote(pg, hpre.at[0], (hs, hr), 6, rows[0]), halos)
    start(remote(pg, hpre.at[1], (hs, hr), 7, rows[1]), halos)

    cap_out[...] = joined(*[dot_nt(hcat[...], wide2[:, b * 768 : (b + 1) * 768]) for b in range(3)]).astype(BF16)

    swap1[3].wait_recv()
    total = keep1[x] + rc1[x].astype(F32)
    for d in range(3):
        sent1[d].wait_recv()
        total = total + r1a[d].astype(F32)
    for n in range(8):
        k1[n] = total[:, n * 4 : (n + 1) * 4]
        s1b[n] = k1[n].astype(BF16)
    next1 = {}
    for d in FAR8:
        start_at(remote(s1b.at[(y + d + 1) % 8], r1b.at[d], (bs, br), 7 + d, ypeers[d]), next1, d)

    for copy in halos[6:8]:
        copy.wait_recv()
    three = [live(hpre[0], -1), pg[...], live(hpre[1], 1)]
    sums = []
    for b in range(3):
        total = None
        for a in range(3):
            at = ((2 - b) * 3 + (2 - a)) * 128
            part = dot(three[a], wide1[:, at : at + 128])
            total = part if total is None else total + part
        sums.append(total)
    in_grad[...] = joined(*sums).astype(BF16)

    t2 = k2[y]
    for d in range(7):
        next2[d].wait_recv()
        t2 = t2 + r2b[d].astype(F32)
    t1 = k1[y]
    for d in range(7):
        next1[d].wait_recv()
        t1 = t1 + r1b[d].astype(F32)
    quarter = lax.broadcasted_iota(jnp.int32, (8, 128), 1) >> 5
    for n in range(2):
        kc[n, :, 0:4] = t2[:, n * 4 : (n + 1) * 4]
        kc[n, :, 4:6] = t1[:, n * 2 : (n + 1) * 2]
        kc[n, :, 6:8] = jnp.zeros((9, 2, 128), F32)
        turned = [
            [kc[n, tap] if turn == 0 else pltpu.roll(kc[n, tap], turn * 32, 1) for turn in range(4)]
            for tap in range(9)
        ]
        for h in range(4):
            for g in range(3):
                packed = turned[g * 4][(4 - h) % 4]
                for k in range(1, 4 if g < 2 else 1):
                    packed = jnp.where(quarter == k, turned[g * 4 + k][(k - h) % 4], packed)
                kp[n, h, g] = packed
            sc[n, h] = kp[n, h].astype(BF16)
    last = {}
    for d in FAR8:
        start_at(remote(sc.at[zto[d] % 2, zto[d] // 2], rcz.at[d], (fs, fr), d, zpeers[d]), last, d)
    total = kp[p["zl"], p["zh"]]
    for d in range(7):
        last[d].wait_recv()
        total = total + rcz[d].astype(F32)
    total = total * SCALE
    for tap in range(9):
        mine_o = total[tap // 4, :, (tap % 4) * 32 : (tap % 4 + 1) * 32]
        grad2[tap] = mine_o[0:4]
        grad1[tap] = mine_o[4:6]
    for group in first + second + pair + [halos, swap2, swap1, sent2, sent1, next2, next1, last]:
        for copy in group.values() if isinstance(group, dict) else group:
            copy.wait_send()


def fused(cap, grad, w1, w2):
    vmem = pl.BlockSpec(memory_space=pltpu.VMEM)
    dma = pltpu.SemaphoreType.DMA
    scratch = [
        ((4, 8, 1152), BF16), ((4, 8, 2304), BF16), ((32, 8, 1152), BF16), ((32, 8, 2304), BF16),
        ((4, 256, 128), BF16), ((2, 256, 256), BF16), ((2, 256, 256), BF16),
        ((5, 256, 128), BF16), ((256, 384), BF16), ((256, 768), BF16), ((3, 256, 256), BF16),
        ((256, 256), F32), ((256, 256), BF16),
        ((4, 9, 32, 128), F32), ((4, 9, 64, 128), F32), ((4, 9, 32, 128), BF16), ((4, 9, 64, 128), BF16),
        ((4, 9, 32, 128), BF16), ((4, 9, 64, 128), BF16), ((4, 9, 32, 128), BF16), ((4, 9, 64, 128), BF16),
        ((3, 9, 32, 128), BF16), ((3, 9, 64, 128), BF16),
        ((8, 9, 4, 128), F32), ((8, 9, 8, 128), F32), ((8, 9, 4, 128), BF16), ((8, 9, 8, 128), BF16),
        ((7, 9, 4, 128), BF16), ((7, 9, 8, 128), BF16),
        ((2, 9, 8, 128), F32), ((2, 4, 3, 8, 128), F32), ((2, 4, 3, 8, 128), BF16), ((7, 3, 8, 128), BF16),
    ]
    sems = [(2,)]
    for shape in ((8,), (2, 3), (2, 9), (2, 13), (8,), (6,), (14,), (7,)):
        sems += [shape, shape]
    return pl.pallas_call(
        fused_kernel,
        out_shape=(
            jax.ShapeDtypeStruct((256, 256), BF16),
            jax.ShapeDtypeStruct((256, 128), BF16),
            jax.ShapeDtypeStruct((9, 2, 32), F32),
            jax.ShapeDtypeStruct((9, 4, 32), F32),
        ),
        in_specs=[vmem] * 4,
        out_specs=(vmem,) * 4,
        scratch_shapes=[pltpu.VMEM(shape, kind) for shape, kind in scratch] + [dma(shape) for shape in sems],
        compiler_params=pltpu.CompilerParams(
            collective_id=0, has_side_effects=True, vmem_limit_bytes=VMEM_BYTES
        ),
        name="fused",
    )(cap, grad, w1, w2)


def hand_over(*arrays):
    def kernel(*refs):
        for source, target in zip(refs[: len(arrays)], refs[len(arrays) :]):
            target[...] = source[...]

    vmem = pl.BlockSpec(memory_space=pltpu.VMEM)
    return pl.pallas_call(
        kernel,
        out_shape=tuple(jax.ShapeDtypeStruct(v.shape, v.dtype) for v in arrays),
        in_specs=[vmem] * len(arrays),
        out_specs=(vmem,) * len(arrays),
        name="hand_over",
    )(*arrays)


def body(cap_in, conv1_weight, conv2_weight, out_grad):
    cap_out, in_grad, grad1, grad2 = fused(
        cap_in.reshape(256, 128), out_grad.reshape(256, 256),
        jnp.transpose(conv1_weight, (0, 1, 3, 2)), jnp.transpose(conv2_weight, (0, 1, 3, 2)),
    )
    cap_out, in_grad, grad1, grad2 = hand_over(cap_out, in_grad, grad1, grad2)
    return (
        cap_out.reshape(1, 1, 256, 256),
        in_grad.reshape(1, 1, 256, 128),
        jnp.transpose(grad1.reshape(3, 3, 2, 32), (3, 0, 1, 2)),
        jnp.transpose(grad2.reshape(3, 3, 4, 32), (3, 0, 1, 2)),
    )


def solution(mesh):
    placed = (
        P("fsdp", "tile", None, None),
        P(None, None, None, "fsdp"),
        P(None, None, None, "fsdp"),
        P("fsdp", "tile", None, None),
    )
    return jax.shard_map(
        body,
        mesh=mesh,
        in_specs=placed,
        out_specs=(
            P("fsdp", "tile", None, None),
            P("fsdp", "tile", None, None),
            P("fsdp", None, None, "tile"),
            P("fsdp", None, None, "tile"),
        ),
        check_vma=False,
    )
```
